32 devices in a mesh: frames: 8 (over z, x), rows: 4 (over y, core).
Axes of the slice: x: 2, y: 2, z: 4, core: 2. Of those that a mesh axis runs over, the one named last changes fastest.
Arguments:
- latent: bfloat16 [8, 32, 128, 512], P('frames', 'rows'), may hold values from -20 to 20, as said below
- norm_gain: float32 [512], replicated, may hold values from 0.1 to 1.9
- norm_shift: float32 [512], replicated, may hold values from -3 to 3
- conv_one: bfloat16 [3, 3, 512, 512], replicated, may hold values from -0.09375 to 0.09375
- bias_one: float32 [512], replicated, may hold values from -3 to 3
- conv_two: bfloat16 [3, 3, 512, 256], replicated, may hold values from -0.09375 to 0.09375
- bias_two: float32 [256], replicated, may hold values from -3 to 3
- temporal_weight: bfloat16 [3, 256, 256], replicated, may hold values from -0.21875 to 0.21875
- bias_temporal: float32 [256], replicated, may hold values from -3 to 3
- clip_ids: int32 [8], replicated, may hold values from 0 to 3, never falling along the last dimension, each value on 1 to 4 neighbouring positions
Outputs:
- decoded: bfloat16 [8, 64, 256, 256], P(None, 'rows', 'frames')
The draws below stay inside these ranges and needn't reach their ends.
Inputs may be any that keep to these rules, and one draw needn't show every extreme that they name: latent is of order one; its scale varies over rows and channels. `clip_ids`: clip numbers never fall along the frames; each clip has 1 to 4 frames and one has exactly 4.
All inputs are finite; a program needn't handle non-finite values.
Results may differ from the reference program's by a relative error of at most 0.006.
Values may be sent and summed in bfloat16 or wider, within the bound.
No kernel may reach another device: no remote copies, remote signals or barrier semaphores. Data moves between devices by JAX's collectives and lax.ppermute only.
A program may use at most 64 MiB of HBM per device.

```python
import math
import jax
import jax.numpy as jnp
import numpy as np
from jax import lax

C1 = 512
C2 = 256
GROUPS = 32
TEMPORAL_TAPS = 3
FRAME_DILATION = 2
WL = 128
CLIPS = 4
F = 8
LOW_H = 32


def draw_latent(key, part):
    key_base, key_chan = jax.random.split(jax.random.fold_in(key, 11), 2)
    height = jnp.arange(LOW_H, dtype=jnp.float32)
    ramp = 3.0 ** (height / max(LOW_H - 1, 1))
    channel_scale = jnp.exp(jax.random.uniform(key_chan, (C1,), jnp.float32, jnp.log(0.5), jnp.log(2.0)))
    base = jnp.clip(jax.random.normal(key_base, (F, LOW_H, WL, C1), jnp.float32), -4.0, 4.0)
    scaled = 0.7 * base * ramp[None, :, None, None] * channel_scale[None, None, None, :]
    return scaled.astype(jnp.bfloat16)


def profile(count, total, bound, slope):
    portions = [(1 << 20) // math.isqrt(rank ** slope) + 1 for rank in range(2, count + 1)]
    spare, given = total - bound - (count - 1), [1] * (count - 1)
    while spare > 0:
        movable = [i for i in range(count - 1) if given[i] < bound]
        pool, budget = sum([portions[i] for i in movable]), spare
        for i in movable:
            extra = min(bound - given[i], max(1, budget * portions[i] // pool), spare)
            given[i] = given[i] + extra
            spare = spare - extra
    return np.array([bound] + given)


def uneven(rng, number_of, total, bound, lean):
    if number_of == 2:
        one = jax.random.randint(rng, (), max(1, total - bound), min(bound, total - 1) + 1)
        return jnp.stack([one, total - one])
    sizes = jnp.asarray(profile(number_of, total, bound, lean), jnp.int32)
    twos = (number_of - 1) // 2
    giver, taker = sizes[1:1 + 2 * twos:2], sizes[2:2 + 2 * twos:2]
    room = jnp.minimum(giver - 1, bound - taker)
    moved = jax.random.randint(jax.random.fold_in(rng, 1), (twos,), 0, 1 << 20) % (room + 1)
    sizes = sizes.at[1:1 + 2 * twos:2].set(giver - moved).at[2:2 + 2 * twos:2].set(taker + moved)
    return sizes[jax.random.permutation(jax.random.fold_in(rng, 2), number_of)]


def scatter_about(rng, shape, deviation, bound, held_as=jnp.bfloat16):
    array = jax.random.normal(rng, shape, jnp.float32) * deviation
    return jnp.minimum(jnp.maximum(array, -bound), bound).astype(held_as)


def setup_inputs(seed: int = 0) -> dict:
    key_of = jax.random.split(jax.random.key(seed), 11)
    latent = draw_latent(jax.random.fold_in(key_of[10], 71), 0)
    norm_gain = jnp.clip(1.0 + 0.18 * jax.random.normal(key_of[1], (C1,), jnp.float32), 0.1, 1.9)
    norm_shift = scatter_about(key_of[2], (C1,), 0.5, 3.0, jnp.float32)
    conv_one = scatter_about(key_of[3], (3, 3, C1, C1), (9 * C1) ** -0.5, 0.09375)
    bias_one = scatter_about(key_of[4], (C1,), 0.5, 3.0, jnp.float32)
    conv_two = scatter_about(key_of[5], (3, 3, C1, C2), (9 * C1) ** -0.5, 0.09375)
    bias_two = scatter_about(key_of[6], (C2,), 0.5, 3.0, jnp.float32)
    temporal_weight = scatter_about(key_of[7], (TEMPORAL_TAPS, C2, C2), (TEMPORAL_TAPS * C2) ** -0.5, 0.21875)
    bias_temporal = scatter_about(key_of[8], (C2,), 0.5, 3.0, jnp.float32)
    clip_ids = jnp.searchsorted(jnp.cumsum(uneven(key_of[9], CLIPS, F, F // 2, 2)), jnp.arange(F), side="right").astype(jnp.int32)
    return dict(latent=latent, norm_gain=norm_gain, norm_shift=norm_shift, conv_one=conv_one, bias_one=bias_one, conv_two=conv_two, bias_two=bias_two, temporal_weight=temporal_weight, bias_temporal=bias_temporal, clip_ids=clip_ids)


GN_EPS = 1e-06

def convolve(picture, weights):
    result = lax.conv_general_dilated(picture.astype(jnp.float32)[None], weights.astype(jnp.float32), (1, 1), ((1, 1), (1, 1)), dimension_numbers=('NHWC', 'HWIO', 'NHWC'), precision=lax.Precision.HIGHEST)
    return result[0]

def clip_starts(clip_ids):
    frame_positions = jnp.arange(clip_ids.shape[0], dtype=jnp.int32)
    same_clip = clip_ids[:, None] == clip_ids[None, :]
    return lax.optimization_barrier(jnp.min(jnp.where(same_clip, frame_positions[None, :], clip_ids.shape[0]), axis=1)).astype(jnp.int32)

def reference(latent, norm_gain, norm_shift, conv_one, bias_one, conv_two, bias_two, temporal_weight, bias_temporal, clip_ids):

    def spatial(frame):
        height, width, channels = frame.shape
        value_rows = frame.astype(jnp.float32).reshape(height * width, GROUPS, channels // GROUPS)
        group_average = lax.optimization_barrier(jnp.mean(value_rows, axis=(0, 2)))
        group_meansq = lax.optimization_barrier(jnp.mean(value_rows * value_rows, axis=(0, 2)))
        variance = group_meansq - group_average * group_average
        normed = (value_rows - group_average[None, :, None]) * lax.rsqrt(variance + GN_EPS)[None, :, None]
        normed = normed.reshape(height, width, channels) * norm_gain + norm_shift
        hidden = jax.nn.silu(normed).astype(jnp.bfloat16)
        first = (convolve(hidden, conv_one) + bias_one).astype(jnp.bfloat16)
        enlarged = jnp.repeat(jnp.repeat(first, 2, axis=0), 2, axis=1)
        return (convolve(enlarged, conv_two) + bias_two).astype(jnp.bfloat16)
    second = lax.map(spatial, latent)
    start_offsets = clip_starts(clip_ids)
    frame_positions = jnp.arange(clip_ids.shape[0], dtype=jnp.int32)
    source_frames = [jnp.maximum(frame_positions - tap_index * FRAME_DILATION, start_offsets).astype(jnp.int32) for tap_index in range(TEMPORAL_TAPS)]

    def temporal(image_row):
        activated = jax.nn.silu(image_row.astype(jnp.float32)).astype(jnp.bfloat16)
        branch = jnp.zeros(image_row.shape, jnp.float32)
        for tap_index in range(TEMPORAL_TAPS):
            chosen = jnp.take(activated, source_frames[tap_index], axis=0)
            branch = branch + jnp.einsum('fwc,cd->fwd', chosen.astype(jnp.float32), temporal_weight[tap_index].astype(jnp.float32))
        return (image_row.astype(jnp.float32) + bias_temporal + branch).astype(jnp.bfloat16)
    result = lax.map(temporal, jnp.swapaxes(second, 0, 1))
    return jnp.swapaxes(result, 0, 1)
```

```python
import functools

import jax
import jax.numpy as jnp
from jax import lax
from jax.experimental import pallas as pl
from jax.experimental.pallas import tpu as pltpu
from jax.sharding import PartitionSpec as P

GROUPS = 32
TAPS = 3
DILATION = 2
GN_EPS = 1e-06
BF16, F32 = jnp.bfloat16, jnp.float32


class Plan:
    def __init__(self, frames, rows, cols, c1, c2):
        self.F, self.R, self.C, self.c1, self.c2 = frames, rows, cols, c1, c2
        self.CH = cols + 4
        self.G = max(1, 16 // frames)
        self.S = self.G * frames
        self.halo = -(-2 * self.CH // 16) * 16
        self.q = max(1, 16 // (2 * cols))
        self.cells = 2 * rows * 2 * cols


def silu(v):
    return v / (1.0 + jnp.exp(-v))


def dot(a, b):
    return jnp.dot(a, b, preferred_element_type=F32)


def stage_kernel(
    p, src, edge, recv, top, bot, w1_hbm, w2_hbm, wt, b1, b2, bt, pin, pout, out,
    cells, even, odd, feven, fodd, phase, second, act, w1, w2, sems,
):
    F, R, C, CH, G, S, c1, c2 = p.F, p.R, p.C, p.CH, p.G, p.S, p.c1, p.c2
    copy1 = pltpu.make_async_copy(w1_hbm, w1, sems.at[0])
    copy2 = pltpu.make_async_copy(w2_hbm, w2, sems.at[1])
    copy1.start()
    copy2.start()

    def turn(ref, first, count, at):
        for j in range(count // 16):
            block = jnp.concatenate([ref[f, 16 * j : 16 * j + 16, :] for f in range(F)], axis=0)
            turned = dot(pin[...], block).reshape(16, F, c1)
            lo = max(first - 16 * j, 0)
            cells[at + 16 * j + lo - first : at + 16 * j + 16 - first] = turned[lo:]

    skip = p.halo - 2 * CH
    turn(bot, 0, p.halo, (R + 2) * CH)
    turn(recv, 0, R * CH, 2 * CH)
    turn(top, skip, p.halo, 0)

    def split(r, carry):
        row = cells[pl.ds(r * CH, CH)]
        even[r] = row.reshape(CH // G, S, c1).astype(BF16)
        if G == 2:
            odd[r] = row[1 : CH - 1].reshape(CH // G - 1, S, c1).astype(BF16)
        return carry

    lax.fori_loop(0, R + 4, split, 0)

    def piece(e, o, r, nr, dc, n):
        if G == 1:
            v = e[pl.ds(r, nr), dc : dc + n]
        elif dc == 1:
            v = o[pl.ds(r, nr), 0:n]
        else:
            v = e[pl.ds(r, nr), dc // 2 : dc // 2 + n]
        return v.reshape(nr * n * S, v.shape[-1])

    n1 = (C + 2) // G
    nr1 = 2
    copy1.wait()
    left = edge[2]
    right = edge[3]

    def conv_one(i, carry):
        r = i * nr1
        acc = None
        for dr in range(3):
            for dc in range(3):
                t = dot(piece(even, odd, r + dr, nr1, dc, n1), w1[dr * 3 + dc])
                acc = t if acc is None else acc + t
        v = (acc + b1[...]).reshape(nr1, C + 2, F, c1)
        for k in range(nr1):
            row_in = jnp.logical_and(r + k >= edge[0], r + k < edge[1])
            col = lax.broadcasted_iota(jnp.int32, (C + 2, F, c1), 0)
            keep = jnp.logical_and(jnp.logical_and(col >= left, col < right), row_in)
            row = jnp.where(keep, v[k], 0.0)
            feven[r + k] = row.reshape(n1, S, c1).astype(BF16)
            if G == 2:
                fodd[r + k] = row[1 : C + 1].reshape(n1 - 1, S, c1).astype(BF16)
        return carry

    lax.fori_loop(0, (R + 2) // nr1, conv_one, 0)

    n2 = C // G
    nr2 = min(R, 4)
    copy2.wait()

    def conv_two(i, carry):
        r = i * nr2
        for a in range(2):
            for b in range(2):
                acc = None
                for da in range(2):
                    for db in range(2):
                        lhs = piece(feven, fodd, r + a + da, nr2, b + db, n2)
                        t = dot(lhs, w2[((a * 2 + b) * 2 + da) * 2 + db])
                        acc = t if acc is None else acc + t
                phase[a, b, pl.ds(r, nr2)] = (acc + b2[...]).astype(BF16).reshape(nr2, C * F, c2)
        return carry

    lax.fori_loop(0, R // nr2, conv_two, 0)

    for blk in range(2 * R // p.q):
        rows = range(blk * p.q, blk * p.q + p.q)
        x = jnp.concatenate([phase[o % 2, b, o // 2] for o in rows for b in range(2)], axis=0)
        turned = dot(pout[...], x)
        at = blk * p.q * 2 * C
        n = p.q * 2 * C
        second[:, at : at + n, :] = turned.astype(BF16).reshape(F, n, c2)
        act[:, at : at + n, :] = silu(turned).astype(BF16).reshape(F, n, c2)

    def temporal(t, carry):
        lhs = jnp.concatenate([act[src[k, t]] for k in range(TAPS)], axis=-1)
        out[t] = (dot(lhs, wt[...]) + second[t].astype(F32) + bt[...]).astype(BF16)
        return carry

    lax.fori_loop(0, F, temporal, 0)


def fused(p, src, edge, recv, top, bot, w1, w2, wt, b1, b2, bt):
    F, R, C, CH, G, S, c1, c2 = p.F, p.R, p.C, p.CH, p.G, p.S, p.c1, p.c2
    ri = jnp.arange(16 * F)
    pin = ((ri[:, None] // F == ri[None, :] % 16) & (ri[:, None] % F == ri[None, :] // 16)).astype(BF16)
    q = p.q
    ro = jnp.arange(q * 2 * C * F)
    of, orow, oc = ro // (q * 2 * C), ro // (2 * C) % q, ro % (2 * C)
    irow, ib, ic, if_ = ro // (2 * C * F), ro // (C * F) % 2, ro // F % C, ro % F
    pout = (
        (of[:, None] == if_[None, :]) & (orow[:, None] == irow[None, :])
        & (oc[:, None] == (2 * ic + ib)[None, :])
    ).astype(BF16)
    vm = pl.BlockSpec(memory_space=pltpu.VMEM)
    sm = pl.BlockSpec(memory_space=pltpu.SMEM)
    hbm = pl.BlockSpec(memory_space=pl.ANY)
    odd_rows = 1 if G == 1 else R + 4
    fodd_rows = 1 if G == 1 else R + 2
    return pl.pallas_call(
        functools.partial(stage_kernel, p),
        out_shape=jax.ShapeDtypeStruct((F, p.cells, c2), BF16),
        in_specs=[sm, sm, vm, vm, vm, hbm, hbm, vm, vm, vm, vm, vm, vm],
        out_specs=vm,
        scratch_shapes=[
            pltpu.VMEM(((R + 4) * CH + p.halo, F, c1), F32),
            pltpu.VMEM((R + 4, CH // G, S, c1), BF16),
            pltpu.VMEM((odd_rows, CH // G - 1, S, c1), BF16),
            pltpu.VMEM((R + 2, (C + 2) // G, S, c1), BF16),
            pltpu.VMEM((fodd_rows, max(1, (C + 2) // G - 1), S, c1), BF16),
            pltpu.VMEM((2, 2, R, C * F, c2), BF16),
            pltpu.VMEM((F, p.cells, c2), BF16),
            pltpu.VMEM((F, p.cells, c2), BF16),
            pltpu.VMEM(w1.shape, BF16),
            pltpu.VMEM(w2.shape, BF16),
            pltpu.SemaphoreType.DMA((2,)),
        ],
        compiler_params=pltpu.CompilerParams(vmem_limit_bytes=60 * 2**20),
    )(src, edge, recv, top, bot, w1, w2, wt, b1, b2, bt, pin, pout)


def clip_starts(clip_ids):
    frame_positions = jnp.arange(clip_ids.shape[0], dtype=jnp.int32)
    same_clip = clip_ids[:, None] == clip_ids[None, :]
    return jnp.min(jnp.where(same_clip, frame_positions[None, :], clip_ids.shape[0]), axis=1)


def phase_weights(conv_two):
    w = conv_two.astype(F32)
    rows = [[w[0], w[1] + w[2]], [w[0] + w[1], w[2]]]
    out = []
    for a in range(2):
        for b in range(2):
            for da in range(2):
                u = rows[a][da]
                pair = [u[0], u[1] + u[2]] if b == 0 else [u[0] + u[1], u[2]]
                out += pair
    return jnp.stack(out).astype(BF16)


def per_device(
    latent, norm_gain, norm_shift, conv_one, bias_one, conv_two, bias_two,
    temporal_weight, bias_temporal, clip_ids,
):
    frames_here, height, width, channels = latent.shape
    c2 = conv_two.shape[-1]
    peers, row_peers = lax.axis_size("frames"), lax.axis_size("rows")
    total_frames = clip_ids.shape[0]
    p = Plan(total_frames, height, width // peers, channels, c2)
    x = latent.astype(F32)
    sums = jnp.sum(x, axis=(1, 2)).reshape(frames_here, GROUPS, -1).sum(-1)
    squares = jnp.sum(x * x, axis=(1, 2)).reshape(frames_here, GROUPS, -1).sum(-1)
    sums, squares = lax.psum((sums, squares), "rows")
    count = height * width * (channels // GROUPS) * row_peers
    mean = sums / count
    inv = lax.rsqrt(squares / count - mean * mean + GN_EPS)
    mean = jnp.repeat(mean, channels // GROUPS, axis=1)[:, None, None, :]
    inv = jnp.repeat(inv, channels // GROUPS, axis=1)[:, None, None, :]
    hidden = jax.nn.silu((x - mean) * inv * norm_gain + norm_shift).astype(BF16)
    padded = jnp.pad(hidden, ((0, 0), (0, 0), (2, 2), (0, 0)))
    send = jnp.stack([padded[:, :, d * p.C : d * p.C + p.CH] for d in range(peers)])
    send = send.reshape(peers * frames_here, height * p.CH, channels)
    recv = lax.all_to_all(send, "frames", split_axis=0, concat_axis=0, tiled=True)
    n = height * p.CH
    top = lax.ppermute(recv[:, n - p.halo :], "rows", [(i, i + 1) for i in range(row_peers - 1)])
    bot = lax.ppermute(recv[:, : p.halo], "rows", [(i + 1, i) for i in range(row_peers - 1)])
    start = clip_starts(clip_ids)
    at = jnp.arange(total_frames, dtype=jnp.int32)
    src = jnp.stack([jnp.maximum(at - k * DILATION, start) for k in range(TAPS)])
    d, r = lax.axis_index("frames"), lax.axis_index("rows")
    edge = jnp.stack([
        jnp.where(r == 0, 1, 0), jnp.where(r == row_peers - 1, height + 1, height + 2),
        jnp.where(d == 0, 1, 0), jnp.where(d == peers - 1, p.C + 1, p.C + 2),
    ]).astype(jnp.int32)
    out = fused(
        p, src, edge, recv, top, bot, conv_one.reshape(9, channels, channels),
        phase_weights(conv_two), temporal_weight.reshape(TAPS * c2, c2),
        bias_one[None], bias_two[None], bias_temporal[None],
    )
    return out.reshape(total_frames, 2 * height, 2 * p.C, c2)


def solution(mesh):
    in_specs = (P("frames", "rows", None, None), P(), P(), P(), P(), P(), P(), P(), P(), P())
    out_specs = P(None, "rows", "frames", None)
    return jax.shard_map(
        per_device, mesh=mesh, in_specs=in_specs, out_specs=out_specs, check_vma=False
    )
```

```python
import functools

import jax
import jax.numpy as jnp
from jax import lax
from jax.experimental import pallas as pl
from jax.experimental.pallas import tpu as pltpu
from jax.sharding import PartitionSpec as P

GROUPS = 32
TAPS = 3
DILATION = 2
GN_EPS = 1e-06
BF16, F32 = jnp.bfloat16, jnp.float32


def up_to(n, m):
    return -(-n // m) * m


class Plan:
    def __init__(self, frames, rows, cols, width, c1, c2, row_peers):
        self.F, self.R, self.C, self.W, self.c1, self.c2 = frames, rows, cols, width, c1, c2
        self.row_peers = row_peers
        self.peers = width // cols
        self.CH = cols + 4
        self.G = max(1, 16 // frames)
        self.S = self.G * frames
        self.T = up_to(2 * self.CH, 8)
        self.NA = 2 * self.T + 8
        self.NB = up_to((rows - 4) * self.CH, 16)
        self.q = max(1, 16 // (2 * cols))
        self.cells = 2 * rows * 2 * cols
        self.swap = self.peers <= 8 and cols % 16 == 0


def silu(v):
    h = 0.5 * v
    return h + h * jnp.tanh(h)


def dot(a, b, **kw):
    return jnp.dot(a, b, preferred_element_type=F32, **kw)


def log2(n):
    assert n & (n - 1) == 0
    return n.bit_length() - 1


def div(x, n):
    return lax.shift_right_logical(x, log2(n))


def mod(x, n):
    return x & (n - 1)


def pack_kernel(p, lat, outer, *inner):
    R, C, W, CH, T = p.R, p.C, p.W, p.CH, p.T

    def row_static(r, dest):
        lo, hi = dest * C - 2, dest * C - 2 + CH
        v = lat[r, max(lo, 0) : min(hi, W), :]
        parts = []
        if lo < 0:
            parts.append(jnp.zeros((-lo, p.c1), BF16))
        parts.append(v)
        if hi > W:
            parts.append(jnp.zeros((hi - W, p.c1), BF16))
        return jnp.concatenate(parts, axis=0) if len(parts) > 1 else v

    def row_dynamic(r, dest):
        at = pl.multiple_of(dest * C, 16)
        before = pl.multiple_of(jnp.maximum(at - 16, 0), 16)
        after = pl.multiple_of(jnp.minimum(at + C, W - 16), 16)
        return jnp.concatenate(
            [lat[r, pl.ds(before, 16), :][14:], lat[r, pl.ds(at, C), :], lat[r, pl.ds(after, 16), :][:2]],
            axis=0,
        )

    total = jnp.zeros((1, p.c1), F32)
    square = jnp.zeros((1, p.c1), F32)
    for r in range(R):
        x = lat[r].astype(F32)
        total = total + jnp.sum(x, axis=0, keepdims=True)
        square = square + jnp.sum(x * x, axis=0, keepdims=True)
    parts = []
    for s in (total, square):
        high = s.astype(BF16).astype(F32)
        middle = (s - high).astype(BF16).astype(F32)
        parts += [high, middle, s - high - middle]
    parts = jnp.concatenate(parts + [jnp.zeros((2, p.c1), F32)], axis=0).astype(BF16)
    for dest in range(p.peers):
        for r, at in ((0, 0), (1, CH), (R - 2, T + 8), (R - 1, T + 8 + CH)):
            outer[dest, at : at + CH, :] = row_static(r, dest)
        if 2 * CH < T:
            for at in (2 * CH, T + 8 + 2 * CH):
                outer[dest, at : at + T - 2 * CH, :] = jnp.zeros((T - 2 * CH, p.c1), BF16)
        outer[dest, T : T + 8, :] = parts
    me = lax.axis_index("frames")
    for s in range(p.peers):
        for i in range(R - 4):
            if p.swap:
                inner[s][i * CH : i * CH + CH, :] = row_dynamic(2 + i, lax.bitwise_xor(me, s))
            else:
                inner[0][s, i * CH : i * CH + CH, :] = row_static(2 + i, s)
        rest = (R - 4) * CH
        if not p.swap and rest < p.NB:
            inner[0][s, rest : p.NB, :] = jnp.zeros((p.NB - rest, p.c1), BF16)


def pack(p, latent):
    vm = pl.BlockSpec(memory_space=pltpu.VMEM)
    outs = [jax.ShapeDtypeStruct((p.peers, p.NA, p.c1), BF16)]
    if p.swap:
        outs += [jax.ShapeDtypeStruct((p.NB, p.c1), BF16)] * p.peers
    else:
        outs += [jax.ShapeDtypeStruct((p.peers, p.NB, p.c1), BF16)]
    outer, *inner = pl.pallas_call(
        functools.partial(pack_kernel, p),
        out_shape=outs,
        in_specs=[vm],
        out_specs=[vm] * len(outs),
        compiler_params=pltpu.CompilerParams(vmem_limit_bytes=32 * 2**20),
    )(latent)
    return outer, inner


def weights_kernel(w, out):
    u = [[w[3 * i + j].astype(F32) for j in range(3)] for i in range(3)]
    for a in range(2):
        for da in range(2):
            if a == 0:
                row = u[0] if da == 0 else [x + y for x, y in zip(u[1], u[2])]
            else:
                row = u[2] if da == 1 else [x + y for x, y in zip(u[0], u[1])]
            for b in range(2):
                pair = (row[0], row[1] + row[2]) if b == 0 else (row[0] + row[1], row[2])
                for db in range(2):
                    out[((a * 2 + b) * 2 + da) * 2 + db] = pair[db].astype(BF16)


def phase_weights(w):
    taps, c1, c2 = w.shape
    step = 64
    return pl.pallas_call(
        weights_kernel,
        grid=(c1 // step,),
        out_shape=jax.ShapeDtypeStruct((16, c1, c2), BF16),
        in_specs=[pl.BlockSpec((taps, step, c2), lambda i: (0, i, 0))],
        out_specs=pl.BlockSpec((16, step, c2), lambda i: (0, i, 0)),
        compiler_params=pltpu.CompilerParams(vmem_limit_bytes=16 * 2**20),
        cost_estimate=pl.CostEstimate(
            flops=20 * c1 * c2, transcendentals=0, bytes_accessed=50 * c1 * c2
        ),
    )(w)


def main_kernel(p, n_inner, clip, *refs):
    outer, inner = refs[0], refs[1 : 1 + n_inner]
    (above, below, across, gain, shift, w1_hbm, w2_hbm, wt, b1, b2, bt, out,
     cells, even, odd, feven, fodd, phase, second, act, w1, w2, start, sems) = refs[1 + n_inner :]
    F, R, C, CH, G, S, T, c1, c2 = p.F, p.R, p.C, p.CH, p.G, p.S, p.T, p.c1, p.c2
    copy1 = pltpu.make_async_copy(w1_hbm, w1, sems.at[0])
    copy2 = pltpu.make_async_copy(w2_hbm, w2, sems.at[1])
    copy1.start()
    copy2.start()
    me = lax.axis_index("frames")
    my_row = lax.axis_index("rows")

    parts = jnp.concatenate(
        [outer[f, T : T + 8, :].astype(F32) for f in range(F)]
        + [above[f, 0:8, :].astype(F32) for f in range(F)]
        + [below[f, T : T + 8, :].astype(F32) for f in range(F)]
        + [across[k, f].astype(F32) for k in range(p.row_peers - 3) for f in range(F)],
        axis=0,
    ).astype(BF16)
    i = lax.broadcasted_iota(jnp.int32, (2 * F, parts.shape[0]), 0)
    j = lax.broadcasted_iota(jnp.int32, (2 * F, parts.shape[0]), 1)
    kind = mod(j, 8)
    wanted = jnp.where(i < F, jnp.where(kind < 3, 1, 0), jnp.where((kind >= 3) & (kind < 6), 1, 0))
    pick = jnp.where((mod(div(j, 8), F) == mod(i, F)) & (wanted == 1), 1.0, 0.0).astype(BF16)
    sums = dot(pick, parts)
    per_group = c1 // GROUPS
    i = lax.broadcasted_iota(jnp.int32, (c1, c1), 0)
    j = lax.broadcasted_iota(jnp.int32, (c1, c1), 1)
    same = jnp.where(div(i, per_group) == div(j, per_group), 1.0, 0.0).astype(BF16)
    grouped = jnp.zeros((2 * F, c1), F32)
    for _ in range(3):
        term = sums.astype(BF16)
        grouped = grouped + dot(term, same)
        sums = sums - term.astype(F32)
    count = p.row_peers * R * p.W * per_group
    mean = grouped[:F] / count
    variance = grouped[F:] / count - mean * mean
    scale = lax.rsqrt(variance + GN_EPS) * gain[...]
    offset = shift[...] - mean * scale

    def turner(first):
        i = lax.broadcasted_iota(jnp.int32, (16 * F, 16 * F), 0)
        j = lax.broadcasted_iota(jnp.int32, (16 * F, 16 * F), 1)
        frame = lax.bitwise_xor(div(j, 16), first)
        return jnp.where((div(i, F) == mod(j, 16)) & (mod(i, F) == frame), 1.0, 0.0).astype(BF16)

    def turn(load, matrix, block, runs):
        lo_b = block
        turned = None
        for first, count, row in runs:
            lo, hi = max(first, lo_b), min(first + count, lo_b + 16)
            if lo >= hi:
                continue
            if turned is None:
                data = jnp.concatenate([load(f, lo_b) for f in range(F)], axis=0)
                turned = dot(matrix, data).reshape(16, F, c1)
                turned = silu(turned * scale[None] + offset[None])
            at = lo
            while at < hi:
                r, c = divmod(at - first, CH)
                n = min(hi - at, CH - c)
                cells[row + r, c : c + n] = turned[at - lo_b : at - lo_b + n]
                at += n

    plain = turner(0)
    inner_turn = turner(me) if n_inner > 1 else plain
    span = 2 * CH
    for block in sorted({min(b, p.NA - 16) for b in range(0, p.NA, 16)}):
        turn(lambda f, b: outer[f, b : b + 16, :], plain, block, [(0, span, 2), (T + 8, span, R)])
    for block in sorted({min(b, T + 8 - 16) for b in range(0, T + 8, 16)}):
        turn(lambda f, b: above[f, b : b + 16, :], plain, block, [(8, span, 0)])
        turn(lambda f, b: below[f, b : b + 16, :], plain, block, [(0, span, R + 2)])
    for block in range(0, p.NB, 16):
        if n_inner > 1:
            load = lambda f, b: inner[f][b : b + 16, :]
        else:
            load = lambda f, b: inner[0][f, b : b + 16, :]
        turn(load, inner_turn, block, [(0, (R - 4) * CH, 4)])

    @pl.when(me == 0)
    def _():
        cells[:, 0:2] = jnp.zeros((R + 4, 2, F, c1), F32)

    @pl.when(me == p.peers - 1)
    def _():
        cells[:, CH - 2 : CH] = jnp.zeros((R + 4, 2, F, c1), F32)

    @pl.when(my_row == 0)
    def _():
        cells[0:2] = jnp.zeros((2, CH, F, c1), F32)

    @pl.when(my_row == p.row_peers - 1)
    def _():
        cells[R + 2 : R + 4] = jnp.zeros((2, CH, F, c1), F32)

    def split(r, carry):
        even[r] = cells[r].reshape(CH // G, S, c1).astype(BF16)
        if G == 2:
            odd[r] = cells[r, 1 : CH - 1].reshape(CH // G - 1, S, c1).astype(BF16)
        return carry

    lax.fori_loop(0, R + 4, split, 0)

    def piece(e, o, r, nr, dc, n):
        if G == 1:
            v = e[pl.ds(r, nr), dc : dc + n]
        elif dc == 1:
            v = o[pl.ds(r, nr), 0:n]
        else:
            v = e[pl.ds(r, nr), dc // 2 : dc // 2 + n]
        return v.reshape(nr * n * S, v.shape[-1])

    n1 = (C + 2) // G
    nr1 = 2
    copy1.wait()
    left = jnp.where(me == 0, 1, 0)
    right = jnp.where(me == p.peers - 1, C + 1, C + 2)
    upper = jnp.where(my_row == 0, 1, 0)
    lower = jnp.where(my_row == p.row_peers - 1, R + 1, R + 2)

    def conv_one(i, carry):
        r = i * nr1
        acc = None
        for dr in range(3):
            for dc in range(3):
                t = dot(piece(even, odd, r + dr, nr1, dc, n1), w1[dr * 3 + dc])
                acc = t if acc is None else acc + t
        v = (acc + b1[...]).reshape(nr1, C + 2, F, c1)
        for k in range(nr1):
            row_in = jnp.logical_and(r + k >= upper, r + k < lower)
            col = lax.broadcasted_iota(jnp.int32, (C + 2, F, c1), 0)
            keep = jnp.logical_and(jnp.logical_and(col >= left, col < right), row_in)
            row = jnp.where(keep, v[k], 0.0)
            feven[r + k] = row.reshape(n1, S, c1).astype(BF16)
            if G == 2:
                fodd[r + k] = row[1 : C + 1].reshape(n1 - 1, S, c1).astype(BF16)
        return carry

    lax.fori_loop(0, (R + 2) // nr1, conv_one, 0)

    n2 = C // G
    nr2 = min(R, 4)
    copy2.wait()

    def conv_two(i, carry):
        r = i * nr2
        for a in range(2):
            for b in range(2):
                acc = None
                for da in range(2):
                    for db in range(2):
                        lhs = piece(feven, fodd, r + a + da, nr2, b + db, n2)
                        t = dot(lhs, w2[((a * 2 + b) * 2 + da) * 2 + db])
                        acc = t if acc is None else acc + t
                phase[a, b, pl.ds(r, nr2)] = (acc + b2[...]).astype(BF16).reshape(nr2, C * F, c2)
        return carry

    lax.fori_loop(0, R // nr2, conv_two, 0)

    q = p.q
    n = q * 2 * C
    i = lax.broadcasted_iota(jnp.int32, (n * F, n * F), 0)
    j = lax.broadcasted_iota(jnp.int32, (n * F, n * F), 1)
    source_cell = div(j, 2 * C * F) * (2 * C) + 2 * mod(div(j, F), C) + mod(div(j, C * F), 2)
    back = jnp.where((div(i, n) == mod(j, F)) & (mod(i, n) == source_cell), 1.0, 0.0).astype(BF16)
    for blk in range(2 * R // q):
        rows = range(blk * q, blk * q + q)
        x = jnp.concatenate([phase[o % 2, b, o // 2] for o in rows for b in range(2)], axis=0)
        turned = dot(back, x)
        second[:, blk * n : blk * n + n, :] = turned.astype(BF16).reshape(F, n, c2)
        act[:, blk * n : blk * n + n, :] = silu(turned).astype(BF16).reshape(F, n, c2)

    start[0] = 0

    def find(t, carry):
        start[t] = jnp.where(clip[t] == clip[t - 1], start[t - 1], t)
        return carry

    lax.fori_loop(1, F, find, 0)

    def temporal(t, carry):
        taps = [act[jnp.maximum(t - k * DILATION, start[t])] for k in range(TAPS)]
        lhs = jnp.concatenate(taps, axis=-1)
        out[t] = (dot(lhs, wt[...]) + second[t].astype(F32) + bt[...]).astype(BF16)
        return carry

    lax.fori_loop(0, F, temporal, 0)


def main(p, clip, outer, inner, above, below, across, gain, shift, w1, w2, wt, b1, b2, bt):
    F, R, C, CH, G, S, c1, c2 = p.F, p.R, p.C, p.CH, p.G, p.S, p.c1, p.c2
    vm = pl.BlockSpec(memory_space=pltpu.VMEM)
    sm = pl.BlockSpec(memory_space=pltpu.SMEM)
    hbm = pl.BlockSpec(memory_space=pl.ANY)
    odd_rows = 1 if G == 1 else R + 4
    fodd_rows = 1 if G == 1 else R + 2
    return pl.pallas_call(
        functools.partial(main_kernel, p, len(inner)),
        out_shape=jax.ShapeDtypeStruct((F, p.cells, c2), BF16),
        in_specs=[sm] + [vm] * (1 + len(inner) + 5) + [hbm, hbm] + [vm] * 4,
        out_specs=vm,
        scratch_shapes=[
            pltpu.VMEM((R + 4, CH, F, c1), F32),
            pltpu.VMEM((R + 4, CH // G, S, c1), BF16),
            pltpu.VMEM((odd_rows, CH // G - 1, S, c1), BF16),
            pltpu.VMEM((R + 2, (C + 2) // G, S, c1), BF16),
            pltpu.VMEM((fodd_rows, max(1, (C + 2) // G - 1), S, c1), BF16),
            pltpu.VMEM((2, 2, R, C * F, c2), BF16),
            pltpu.VMEM((F, p.cells, c2), BF16),
            pltpu.VMEM((F, p.cells, c2), BF16),
            pltpu.VMEM(w1.shape, BF16),
            pltpu.VMEM(w2.shape, BF16),
            pltpu.SMEM((F,), jnp.int32),
            pltpu.SemaphoreType.DMA((2,)),
        ],
        compiler_params=pltpu.CompilerParams(vmem_limit_bytes=60 * 2**20),
    )(clip, outer, *inner, above, below, across, gain, shift, w1, w2, wt, b1, b2, bt)


def per_device(
    latent, norm_gain, norm_shift, conv_one, bias_one, conv_two, bias_two,
    temporal_weight, bias_temporal, clip_ids,
):
    _, height, width, c1 = latent.shape
    c2 = conv_two.shape[-1]
    peers, row_peers = lax.axis_size("frames"), lax.axis_size("rows")
    p = Plan(clip_ids.shape[0], height, width // peers, width, c1, c2, row_peers)
    outer, inner = pack(p, latent[0])
    outer = lax.all_to_all(outer, "frames", split_axis=0, concat_axis=0, tiled=True)
    if p.swap:
        order = sorted(range(1, peers), key=lambda s: -(s // 4))
        got = {
            s: lax.ppermute(inner[s], "frames", [(i, i ^ s) for i in range(peers)]) for s in order
        }
        inner = [inner[0]] + [got[s] for s in range(1, peers)]
    else:
        inner = [lax.all_to_all(inner[0], "frames", split_axis=0, concat_axis=0, tiled=True)]

    def over_rows(v, by):
        return lax.ppermute(v, "rows", [(i, (i + by) % row_peers) for i in range(row_peers)])

    above = over_rows(outer[:, p.T :], 1)
    below = over_rows(outer[:, : p.T + 8], -1)
    sums = outer[:, p.T : p.T + 8]
    across = jnp.stack([over_rows(sums, by) for by in range(2, row_peers - 1)])
    out = main(
        p, clip_ids, outer, inner, above, below, across, norm_gain[None], norm_shift[None],
        conv_one.reshape(9, c1, c1), phase_weights(conv_two.reshape(9, c1, c2)),
        temporal_weight.reshape(TAPS * c2, c2), bias_one[None], bias_two[None], bias_temporal[None],
    )
    return out.reshape(p.F, 2 * height, 2 * p.C, c2)


def solution(mesh):
    in_specs = (P("frames", "rows", None, None), P(), P(), P(), P(), P(), P(), P(), P(), P())
    out_specs = P(None, "rows", "frames", None)
    return jax.shard_map(
        per_device, mesh=mesh, in_specs=in_specs, out_specs=out_specs, check_vma=False
    )
```

```python
import functools

import jax
import jax.numpy as jnp
from jax import lax
from jax.experimental import pallas as pl
from jax.experimental.pallas import tpu as pltpu
from jax.sharding import PartitionSpec as P

GROUPS = 32
TAPS = 3
DILATION = 2
GN_EPS = 1e-06
BF16, F32 = jnp.bfloat16, jnp.float32


def up_to(n, m):
    return -(-n // m) * m


class Plan:
    def __init__(self, frames, rows, cols, width, c1, c2, row_peers):
        self.F, self.R, self.C, self.W, self.c1, self.c2 = frames, rows, cols, width, c1, c2
        self.row_peers = row_peers
        self.peers = width // cols
        self.CH = cols + 4
        self.G = max(1, 16 // frames)
        self.S = self.G * frames
        self.T = up_to(2 * self.CH, 8)
        self.NA = 2 * self.T + 8
        self.NB = up_to((rows - 4) * self.CH, 16)
        self.q = max(1, 16 // (2 * cols))
        self.cells = 2 * rows * 2 * cols
        packed = (rows + 4) * self.CH * frames * c1
        self.vmem = 11 * packed + 24 * self.cells * frames * c2 // 2 + 4 * 2**20
        self.near = self.peers // 2
        self.swap = self.peers <= 8 and cols % 16 == 0


def silu(v):
    h = 0.5 * v
    return h + h * jnp.tanh(h)


def dot(a, b, **kw):
    return jnp.dot(a, b, preferred_element_type=F32, **kw)


def log2(n):
    assert n & (n - 1) == 0
    return n.bit_length() - 1


def div(x, n):
    return lax.shift_right_logical(x, log2(n))


def mod(x, n):
    return x & (n - 1)


def messages(p, refs):
    if not p.swap:
        whole = [refs[0].at[f] for f in range(p.peers)]
        return [r.at[: p.NA] for r in whole], [r.at[p.NA :] for r in whole]
    near, far = refs[: p.near], refs[p.near :]
    outer, inner = far[: p.peers - p.near], far[p.peers - p.near :]
    return (
        [r.at[: p.NA] for r in near] + list(outer),
        [r.at[p.NA :] for r in near] + list(inner),
    )


def pack_kernel(p, lat, *refs):
    R, C, W, CH, T = p.R, p.C, p.W, p.CH, p.T
    outer, inner = messages(p, refs)

    def row_static(r, dest):
        lo, hi = dest * C - 2, dest * C - 2 + CH
        v = lat[r, max(lo, 0) : min(hi, W), :]
        parts = []
        if lo < 0:
            parts.append(jnp.zeros((-lo, p.c1), BF16))
        parts.append(v)
        if hi > W:
            parts.append(jnp.zeros((hi - W, p.c1), BF16))
        return jnp.concatenate(parts, axis=0) if len(parts) > 1 else v

    def row_dynamic(r, dest):
        at = pl.multiple_of(dest * C, 16)
        before = pl.multiple_of(jnp.maximum(at - 16, 0), 16)
        after = pl.multiple_of(jnp.minimum(at + C, W - 16), 16)
        return jnp.concatenate(
            [lat[r, pl.ds(before, 16), :][14:], lat[r, pl.ds(at, C), :], lat[r, pl.ds(after, 16), :][:2]],
            axis=0,
        )

    total = jnp.zeros((1, p.c1), F32)
    square = jnp.zeros((1, p.c1), F32)
    for r in range(R):
        x = lat[r].astype(F32)
        total = total + jnp.sum(x, axis=0, keepdims=True)
        square = square + jnp.sum(x * x, axis=0, keepdims=True)
    parts = []
    for s in (total, square):
        high = s.astype(BF16).astype(F32)
        middle = (s - high).astype(BF16).astype(F32)
        parts += [high, middle, s - high - middle]
    parts = jnp.concatenate(parts + [jnp.zeros((2, p.c1), F32)], axis=0).astype(BF16)
    me = lax.axis_index("frames")
    for s in range(p.peers):
        a, b = outer[s], inner[s]
        if p.swap:
            load = functools.partial(row_dynamic, dest=lax.bitwise_xor(me, s))
        else:
            load = functools.partial(row_static, dest=s)
        for r, at in ((0, 0), (1, CH), (R - 2, T + 8), (R - 1, T + 8 + CH)):
            a[at : at + CH, :] = load(r)
        if 2 * CH < T:
            for at in (2 * CH, T + 8 + 2 * CH):
                a[at : at + T - 2 * CH, :] = jnp.zeros((T - 2 * CH, p.c1), BF16)
        a[T : T + 8, :] = parts
        for i in range(R - 4):
            b[i * CH : i * CH + CH, :] = load(2 + i)
        rest = (R - 4) * CH
        if rest < p.NB:
            b[rest : p.NB, :] = jnp.zeros((p.NB - rest, p.c1), BF16)


def pack(p, latent):
    vm = pl.BlockSpec(memory_space=pltpu.VMEM)
    n = p.NA + p.NB
    shapes = [(p.peers, n, p.c1)]
    if p.swap:
        far = p.peers - p.near
        shapes = [(n, p.c1)] * p.near + [(p.NA, p.c1)] * far + [(p.NB, p.c1)] * far
    outs = [jax.ShapeDtypeStruct(s, BF16) for s in shapes]
    return pl.pallas_call(
        functools.partial(pack_kernel, p),
        out_shape=outs,
        in_specs=[vm],
        out_specs=[vm] * len(outs),
        compiler_params=pltpu.CompilerParams(vmem_limit_bytes=32 * 2**20),
    )(latent)


def weights_kernel(w, out):
    u = [[w[3 * i + j].astype(F32) for j in range(3)] for i in range(3)]
    for a in range(2):
        for da in range(2):
            if a == 0:
                row = u[0] if da == 0 else [x + y for x, y in zip(u[1], u[2])]
            else:
                row = u[2] if da == 1 else [x + y for x, y in zip(u[0], u[1])]
            for b in range(2):
                pair = (row[0], row[1] + row[2]) if b == 0 else (row[0] + row[1], row[2])
                for db in range(2):
                    out[((a * 2 + b) * 2 + da) * 2 + db] = pair[db].astype(BF16)


def phase_weights(w):
    taps, c1, c2 = w.shape
    step = 64
    return pl.pallas_call(
        weights_kernel,
        grid=(c1 // step,),
        out_shape=jax.ShapeDtypeStruct((16, c1, c2), BF16),
        in_specs=[pl.BlockSpec((taps, step, c2), lambda i: (0, i, 0))],
        out_specs=pl.BlockSpec((16, step, c2), lambda i: (0, i, 0)),
        compiler_params=pltpu.CompilerParams(vmem_limit_bytes=16 * 2**20),
        cost_estimate=pl.CostEstimate(
            flops=20 * c1 * c2, transcendentals=0, bytes_accessed=50 * c1 * c2
        ),
    )(w)


def face_kernel(p, n, second, *refs):
    outer, _ = messages(p, list(refs[:n]) + [None] * (p.peers - p.near))
    T = p.T
    odd = lax.bitwise_and(lax.axis_index("rows"), 1)
    to_above = odd == (0 if second else 1)
    out = refs[-2] if second else refs[-1]

    @pl.when(to_above)
    def _():
        for f in range(p.F):
            out[f, 0:T] = outer[f][0:T, :]

    @pl.when(jnp.logical_not(to_above))
    def _():
        for f in range(p.F):
            out[f, 0:T] = outer[f][T + 8 : 2 * T + 8, :]

    for f in range(p.F):
        sums = outer[f][T : T + 8, :]
        out[f, T : T + 8] = sums
        if second:
            theirs = refs[n][f, T : T + 8]
            out[f, T + 8 : T + 16] = theirs
            refs[-1][f, 0:8] = sums
            refs[-1][f, 8:16] = theirs


def face(p, got, first=None):
    vm = pl.BlockSpec(memory_space=pltpu.VMEM)
    rows = [p.T + 8] if first is None else [p.T + 16, 16]
    args = list(got) + ([] if first is None else [first])
    out = pl.pallas_call(
        functools.partial(face_kernel, p, len(got), first is not None),
        out_shape=[jax.ShapeDtypeStruct((p.F, r, p.c1), BF16) for r in rows],
        in_specs=[vm] * len(args),
        out_specs=[vm] * len(rows),
        compiler_params=pltpu.CompilerParams(vmem_limit_bytes=16 * 2**20),
        cost_estimate=pl.CostEstimate(flops=1, transcendentals=0, bytes_accessed=1),
    )(*args)
    return out[0] if first is None else out


def turner(p, first):
    F = p.F
    i = lax.broadcasted_iota(jnp.int32, (16 * F, 16 * F), 0)
    j = lax.broadcasted_iota(jnp.int32, (16 * F, 16 * F), 1)
    frame = lax.bitwise_xor(div(j, 16), first)
    return jnp.where((div(i, F) == mod(j, 16)) & (mod(i, F) == frame), 1.0, 0.0).astype(BF16)


def turn(p, load, matrix, scale, offset, block, runs, cells):
    if not any(max(f, block) < min(f + n, block + 16) for f, n, _ in runs):
        return
    data = jnp.concatenate([load(f, block) for f in range(p.F)], axis=0)
    turned = dot(matrix, data).reshape(16, p.F, p.c1)
    turned = silu(turned * scale[None] + offset[None])
    for first, count, row in runs:
        at, hi = max(first, block), min(first + count, block + 16)
        while at < hi:
            r, c = divmod(at - first, p.CH)
            n = min(hi - at, p.CH - c)
            cells[row + r, c : c + n] = turned[at - block : at - block + n]
            at += n


def clear_columns(p, cells, me):
    rows = cells.shape[0]

    @pl.when(me == 0)
    def _():
        cells[:, 0:2] = jnp.zeros((rows, 2, p.F, p.c1), F32)

    @pl.when(me == p.peers - 1)
    def _():
        cells[:, p.CH - 2 : p.CH] = jnp.zeros((rows, 2, p.F, p.c1), F32)


def pair_cells(p, row, even, odd):
    n = row.shape[0]
    even[...] = row.reshape(n // p.G, p.S, p.c1).astype(BF16)
    if p.G == 2:
        odd[...] = row[1 : n - 1].reshape(n // 2 - 1, p.S, p.c1).astype(BF16)


def shifted(p, rows, first, count, dc, n):
    parts = []
    for r in range(first, first + count) if isinstance(first, int) else first:
        even, odd = rows[r]
        if p.G == 1:
            v = even[dc : dc + n]
        elif dc == 1:
            v = odd[0:n]
        else:
            v = even[dc // 2 : dc // 2 + n]
        parts.append(v.reshape(n * p.S, p.c1))
    return jnp.concatenate(parts, axis=0)


def conv_one(p, out_rows, hidden, w1, b1, me, my_row, store):
    F, R, C, c1 = p.F, p.R, p.C, p.c1
    acc = None
    for dr in range(3):
        for dc in range(3):
            lhs = shifted(p, hidden, [r + dr for r in out_rows], 0, dc, (C + 2) // p.G)
            u = dot(lhs, w1[dr, dc])
            acc = u if acc is None else acc + u
    v = (acc + b1[...]).reshape(len(out_rows), C + 2, F, c1)
    left = jnp.where(me == 0, 1, 0)
    right = jnp.where(me == p.peers - 1, C + 1, C + 2)
    col = lax.broadcasted_iota(jnp.int32, (C + 2, F, c1), 0)
    for k, r in enumerate(out_rows):
        keep = (col >= left) & (col < right)
        if r == 0:
            keep = keep & (my_row > 0)
        if r == R + 1:
            keep = keep & (my_row < p.row_peers - 1)
        even, odd = store[r]
        pair_cells(p, jnp.where(keep, v[k], 0.0), even, odd)


def outer_kernel(p, n, *refs):
    outer, _ = messages(p, list(refs[:n]) + [None] * (p.peers - p.near))
    (face1, face2, sums2, gain, shift, w1, b1,
     norm, heven, hodd, feven, fodd, cells, teven, todd) = refs[n:]
    F, R, CH, T, c1 = p.F, p.R, p.CH, p.T, p.c1
    me = lax.axis_index("frames")
    my_row = lax.axis_index("rows")
    xor = me if p.swap else 0

    parts = jnp.concatenate(
        [outer[f][T : T + 8, :].astype(F32) for f in range(F)]
        + [face1[f, T : T + 8, :].astype(F32) for f in range(F)]
        + [face2[f, at : at + 8, :].astype(F32) for at in (T, T + 8) for f in range(F)]
        + [sums2[f, at : at + 8, :].astype(F32) for at in (0, 8) for f in range(F)],
        axis=0,
    ).astype(BF16)
    i = lax.broadcasted_iota(jnp.int32, (2 * F, parts.shape[0]), 0)
    j = lax.broadcasted_iota(jnp.int32, (2 * F, parts.shape[0]), 1)
    kind = mod(j, 8)
    wanted = jnp.where(i < F, jnp.where(kind < 3, 1, 0), jnp.where((kind >= 3) & (kind < 6), 1, 0))
    sent = lax.bitwise_xor(mod(div(j, 8), F), xor)
    pick = jnp.where((sent == mod(i, F)) & (wanted == 1), 1.0, 0.0).astype(BF16)
    sums = dot(pick, parts)
    per_group = c1 // GROUPS
    i = lax.broadcasted_iota(jnp.int32, (c1, c1), 0)
    j = lax.broadcasted_iota(jnp.int32, (c1, c1), 1)
    same = jnp.where(div(i, per_group) == div(j, per_group), 1.0, 0.0).astype(BF16)
    grouped = jnp.zeros((2 * F, c1), F32)
    for _ in range(3):
        term = sums.astype(BF16)
        grouped = grouped + dot(term, same)
        sums = sums - term.astype(F32)
    count = p.row_peers * R * p.W * per_group
    mean = grouped[:F] / count
    variance = grouped[F:] / count - mean * mean
    scale = lax.rsqrt(variance + GN_EPS) * gain[...]
    offset = shift[...] - mean * scale
    norm[0] = scale
    norm[1] = offset

    matrix = turner(p, xor)
    span = 2 * CH
    for block in sorted({min(b, p.NA - 16) for b in range(0, p.NA, 16)}):
        turn(p, lambda f, b: outer[f][b : b + 16, :], matrix, scale, offset, block,
             [(0, span, 2), (T + 8, span, 4)], cells)
    odd = lax.bitwise_and(my_row, 1)
    for block in range(0, span, 16):
        turn(p, lambda f, b: face1[f, b : b + 16, :], matrix, scale, offset, block,
             [(0, span, 6 - 6 * odd)], cells)
        turn(p, lambda f, b: face2[f, b : b + 16, :], matrix, scale, offset, block,
             [(0, span, 6 * odd)], cells)
    clear_columns(p, cells, me)

    @pl.when(my_row == 0)
    def _():
        cells[0:2] = jnp.zeros((2, CH, F, c1), F32)

    @pl.when(my_row == p.row_peers - 1)
    def _():
        cells[6:8] = jnp.zeros((2, CH, F, c1), F32)

    hidden = {}
    for k in range(8):
        if 2 <= k < 6:
            even, odd = heven.at[k - 2], hodd.at[k - 2]
        else:
            even, odd = teven.at[k % 4], todd.at[k % 4]
        pair_cells(p, cells[k], even, odd)
        hidden[k if k < 4 else R + k - 4] = (even, odd)
    rows = [0, 1, R, R + 1]
    store = {r: (feven.at[k], fodd.at[k]) for k, r in enumerate(rows)}
    conv_one(p, rows, hidden, w1, b1, me, my_row, store)


def inner_kernel(p, n, clip, *refs):
    _, inner = messages(p, list(refs[: p.near]) + [None] * (p.peers - p.near) + list(refs[p.near : n])
                        if p.swap else refs[:n])
    (norm, heven, hodd, feven_in, fodd_in, w1, w2, wt, b1, b2, bt, out,
     cells, even, odd, feven, fodd, phase, second, act, start) = refs[n:]
    F, R, C, CH, S, c1, c2 = p.F, p.R, p.C, p.CH, p.S, p.c1, p.c2
    me = lax.axis_index("frames")
    my_row = lax.axis_index("rows")
    scale, offset = norm[0], norm[1]
    matrix = turner(p, me if p.swap else 0)
    for block in range(0, p.NB, 16):
        turn(p, lambda f, b: inner[f][b : b + 16, :], matrix, scale, offset, block,
             [(0, (R - 4) * CH, 0)], cells)
    clear_columns(p, cells, me)
    hidden = {r: (heven.at[k], hodd.at[k]) for k, r in enumerate((2, 3, R, R + 1))}
    for k in range(R - 4):
        hidden[4 + k] = (even.at[k], odd.at[k])
        pair_cells(p, cells[k], even.at[k], odd.at[k])
    first = {r: (feven_in.at[k], fodd_in.at[k]) for k, r in enumerate((0, 1, R, R + 1))}
    inside = {r: (feven.at[r - 2], fodd.at[r - 2]) for r in range(2, R)}
    conv_one(p, list(range(2, R)), hidden, w1, b1, me, my_row, inside)
    first.update(inside)

    for a in range(2):
        for b in range(2):
            acc = None
            for da in range(2):
                for db in range(2):
                    lhs = shifted(p, first, a + da, R, b + db, C // p.G)
                    u = dot(lhs, w2[((a * 2 + b) * 2 + da) * 2 + db])
                    acc = u if acc is None else acc + u
            phase[a, b] = (acc + b2[...]).astype(BF16).reshape(R, C * F, c2)

    q = p.q
    n = q * 2 * C
    i = lax.broadcasted_iota(jnp.int32, (n * F, n * F), 0)
    j = lax.broadcasted_iota(jnp.int32, (n * F, n * F), 1)
    source_cell = div(j, 2 * C * F) * (2 * C) + 2 * mod(div(j, F), C) + mod(div(j, C * F), 2)
    back = jnp.where((div(i, n) == mod(j, F)) & (mod(i, n) == source_cell), 1.0, 0.0).astype(BF16)
    for blk in range(2 * R // q):
        rows = range(blk * q, blk * q + q)
        x = jnp.concatenate([phase[o % 2, b, o // 2] for o in rows for b in range(2)], axis=0)
        turned = dot(back, x)
        second[:, blk * n : blk * n + n, :] = turned.astype(BF16).reshape(F, n, c2)
        act[:, blk * n : blk * n + n, :] = silu(turned).astype(BF16).reshape(F, n, c2)

    start[0] = 0

    def find(t, carry):
        start[t] = jnp.where(clip[t] == clip[t - 1], start[t - 1], t)
        return carry

    lax.fori_loop(1, F, find, 0)

    def temporal(t, carry):
        taps = [act[jnp.maximum(t - k * DILATION, start[t])] for k in range(TAPS)]
        lhs = jnp.concatenate(taps, axis=-1)
        out[t] = (dot(lhs, wt[...]) + second[t].astype(F32) + bt[...]).astype(BF16)
        return carry

    if F <= 8:
        for t in range(F):
            temporal(t, 0)
    else:
        lax.fori_loop(0, F, temporal, 0)


def outer_rows(p, got, face1, face2, sums2, gain, shift, w1, b1):
    F, C, CH, G, S, c1 = p.F, p.C, p.CH, p.G, p.S, p.c1
    vm = pl.BlockSpec(memory_space=pltpu.VMEM)
    pairs = lambda rows, cells: [(rows, cells // G, S, c1), (rows, max(1, cells // G - 1), S, c1)]
    return pl.pallas_call(
        functools.partial(outer_kernel, p, len(got)),
        out_shape=[jax.ShapeDtypeStruct((2, F, c1), F32)]
        + [jax.ShapeDtypeStruct(s, BF16) for s in pairs(4, CH) + pairs(4, C + 2)],
        in_specs=[vm] * (len(got) + 7),
        out_specs=[vm] * 5,
        scratch_shapes=[pltpu.VMEM((8, CH, F, c1), F32)] + [pltpu.VMEM(s, BF16) for s in pairs(4, CH)],
        compiler_params=pltpu.CompilerParams(vmem_limit_bytes=p.vmem),
        cost_estimate=pl.CostEstimate(
            flops=2 * 9 * 4 * (C + 2) * F * c1 * c1, transcendentals=8 * CH * F * c1,
            bytes_accessed=2 * 9 * c1 * c1,
        ),
    )(*got, face1, face2, sums2, gain, shift, w1, b1)


def inner_rows(p, clip, got, norm, hidden, first, w1, w2, wt, b1, b2, bt):
    F, R, C, CH, G, S, c1, c2 = p.F, p.R, p.C, p.CH, p.G, p.S, p.c1, p.c2
    vm = pl.BlockSpec(memory_space=pltpu.VMEM)
    sm = pl.BlockSpec(memory_space=pltpu.SMEM)
    pairs = lambda rows, cells: [(rows, cells // G, S, c1), (rows, max(1, cells // G - 1), S, c1)]
    return pl.pallas_call(
        functools.partial(inner_kernel, p, len(got)),
        out_shape=jax.ShapeDtypeStruct((F, p.cells, c2), BF16),
        in_specs=[sm] + [vm] * (len(got) + 11),
        out_specs=vm,
        scratch_shapes=[pltpu.VMEM((R - 4, CH, F, c1), F32)]
        + [pltpu.VMEM(s, BF16) for s in pairs(R - 4, CH) + pairs(R - 2, C + 2)]
        + [
            pltpu.VMEM((2, 2, R, C * F, c2), BF16),
            pltpu.VMEM((F, p.cells, c2), BF16),
            pltpu.VMEM((F, p.cells, c2), BF16),
            pltpu.SMEM((F,), jnp.int32),
        ],
        compiler_params=pltpu.CompilerParams(vmem_limit_bytes=p.vmem),
        cost_estimate=pl.CostEstimate(
            flops=2 * (9 * (R - 2) * (C + 2) * c1 + 16 * R * C * c2) * F * c1,
            transcendentals=p.cells * F * c2, bytes_accessed=34 * c1 * c1,
        ),
    )(clip, *got, norm, *hidden, *first, w1, w2, wt, b1, b2, bt)


def per_device(
    latent, norm_gain, norm_shift, conv_one_w, bias_one, conv_two, bias_two,
    temporal_weight, bias_temporal, clip_ids,
):
    _, height, width, c1 = latent.shape
    c2 = conv_two.shape[-1]
    peers, row_peers = lax.axis_size("frames"), lax.axis_size("rows")
    p = Plan(clip_ids.shape[0], height, width // peers, width, c1, c2, row_peers)
    got = list(pack(p, latent[0]))
    far = range(p.near, peers)

    def swap(v, s):
        return lax.ppermute(v, "frames", [(i, i ^ s) for i in range(peers)])

    def after(v, k):
        v, got[k] = lax.optimization_barrier((v, got[k]))
        return v

    if p.swap:
        near, one, two = got[: p.near], got[p.near : peers], got[peers:]
        got = near + [swap(v, s) for v, s in zip(one, far)]
        for s in range(1, p.near):
            got[s] = swap(near[s], s)
        two = [swap(after(v, s), s) for v, s in zip(two, far)]
        last = got[: p.near] + two
    else:
        got = [lax.all_to_all(got[0], "frames", split_axis=0, concat_axis=0, tiled=True)]
        last = got

    def over_rows(v, *pairs):
        return lax.ppermute(v, "rows", [(i, j) for a, b in pairs for i, j in ((a, b), (b, a))])

    assert row_peers == 4
    face1 = over_rows(face(p, got), (0, 1), (2, 3))
    face2, sums2 = face(p, got, face1)
    face2, sums2 = over_rows(face2, (1, 2)), over_rows(sums2, (0, 3))
    w1 = conv_one_w.reshape(3, 3, c1, c1)
    norm, *packed = outer_rows(
        p, got, face1, face2, sums2, norm_gain[None], norm_shift[None], w1, bias_one[None]
    )
    out = inner_rows(
        p, clip_ids, last, norm, packed[:2], packed[2:], w1,
        phase_weights(conv_two.reshape(9, c1, c2)), temporal_weight.reshape(TAPS * c2, c2),
        bias_one[None], bias_two[None], bias_temporal[None],
    )
    return out.reshape(p.F, 2 * height, 2 * p.C, c2)


def solution(mesh):
    in_specs = (P("frames", "rows", None, None), P(), P(), P(), P(), P(), P(), P(), P(), P())
    out_specs = P(None, "rows", "frames", None)
    return jax.shard_map(
        per_device, mesh=mesh, in_specs=in_specs, out_specs=out_specs, check_vma=False
    )
```

```python
import functools

import jax
import jax.numpy as jnp
from jax import lax
from jax.experimental import pallas as pl
from jax.experimental.pallas import tpu as pltpu
from jax.sharding import PartitionSpec as P

GROUPS = 32
TAPS = 3
DILATION = 2
GN_EPS = 1e-06
BF16, F32 = jnp.bfloat16, jnp.float32


def up_to(n, m):
    return -(-n // m) * m


class Plan:
    def __init__(self, frames, rows, cols, width, c1, c2, row_peers):
        self.F, self.R, self.C, self.W, self.c1, self.c2 = frames, rows, cols, width, c1, c2
        self.row_peers = row_peers
        self.peers = width // cols
        self.CH = cols + 4
        self.G = max(1, 16 // frames)
        self.S = self.G * frames
        self.T = up_to(2 * self.CH, 8)
        self.NA = 2 * self.T + 8
        self.NB = up_to((rows - 4) * self.CH, 16)
        self.q = max(1, 16 // (2 * cols))
        self.cells = 2 * rows * 2 * cols
        packed = (rows + 4) * self.CH * frames * c1
        self.vmem = 11 * packed + 24 * self.cells * frames * c2 // 2 + 4 * 2**20
        self.near = self.peers // 2
        self.swap = self.peers <= 8 and cols % 16 == 0


def silu(v):
    h = 0.5 * v
    return h + h * jnp.tanh(h)


def dot(a, b, **kw):
    return jnp.dot(a, b, preferred_element_type=F32, **kw)


def log2(n):
    assert n & (n - 1) == 0
    return n.bit_length() - 1


def div(x, n):
    return lax.shift_right_logical(x, log2(n))


def mod(x, n):
    return x & (n - 1)


def messages(p, refs):
    if not p.swap:
        whole = [refs[0].at[f] for f in range(p.peers)]
        return [r.at[: p.NA] for r in whole], [r.at[p.NA :] for r in whole]
    near, far = refs[: p.near], refs[p.near :]
    outer, inner = far[: p.peers - p.near], far[p.peers - p.near :]
    return (
        [r.at[: p.NA] for r in near] + list(outer),
        [r.at[p.NA :] for r in near] + list(inner),
    )


def pack_kernel(p, lat, *refs):
    R, C, W, CH, T = p.R, p.C, p.W, p.CH, p.T
    outer, inner = messages(p, refs)

    def row_static(r, dest):
        lo, hi = dest * C - 2, dest * C - 2 + CH
        v = lat[r, max(lo, 0) : min(hi, W), :]
        parts = []
        if lo < 0:
            parts.append(jnp.zeros((-lo, p.c1), BF16))
        parts.append(v)
        if hi > W:
            parts.append(jnp.zeros((hi - W, p.c1), BF16))
        return jnp.concatenate(parts, axis=0) if len(parts) > 1 else v

    def row_dynamic(r, dest):
        at = pl.multiple_of(dest * C, 16)
        before = pl.multiple_of(jnp.maximum(at - 16, 0), 16)
        after = pl.multiple_of(jnp.minimum(at + C, W - 16), 16)
        return jnp.concatenate(
            [lat[r, pl.ds(before, 16), :][14:], lat[r, pl.ds(at, C), :], lat[r, pl.ds(after, 16), :][:2]],
            axis=0,
        )

    total = jnp.zeros((1, p.c1), F32)
    square = jnp.zeros((1, p.c1), F32)
    for r in range(R):
        x = lat[r].astype(F32)
        total = total + jnp.sum(x, axis=0, keepdims=True)
        square = square + jnp.sum(x * x, axis=0, keepdims=True)
    parts = []
    for s in (total, square):
        high = s.astype(BF16).astype(F32)
        middle = (s - high).astype(BF16).astype(F32)
        parts += [high, middle, s - high - middle]
    parts = jnp.concatenate(parts + [jnp.zeros((2, p.c1), F32)], axis=0).astype(BF16)
    me = lax.axis_index("frames")
    for s in range(p.peers):
        a, b = outer[s], inner[s]
        if p.swap:
            load = functools.partial(row_dynamic, dest=lax.bitwise_xor(me, s))
        else:
            load = functools.partial(row_static, dest=s)
        for r, at in ((0, 0), (1, CH), (R - 2, T + 8), (R - 1, T + 8 + CH)):
            a[at : at + CH, :] = load(r)
        if 2 * CH < T:
            for at in (2 * CH, T + 8 + 2 * CH):
                a[at : at + T - 2 * CH, :] = jnp.zeros((T - 2 * CH, p.c1), BF16)
        a[T : T + 8, :] = parts
        for i in range(R - 4):
            b[i * CH : i * CH + CH, :] = load(2 + i)
        rest = (R - 4) * CH
        if rest < p.NB:
            b[rest : p.NB, :] = jnp.zeros((p.NB - rest, p.c1), BF16)


def pack(p, latent):
    vm = pl.BlockSpec(memory_space=pltpu.VMEM)
    n = p.NA + p.NB
    shapes = [(p.peers, n, p.c1)]
    if p.swap:
        far = p.peers - p.near
        shapes = [(n, p.c1)] * p.near + [(p.NA, p.c1)] * far + [(p.NB, p.c1)] * far
    outs = [jax.ShapeDtypeStruct(s, BF16) for s in shapes]
    return pl.pallas_call(
        functools.partial(pack_kernel, p),
        out_shape=outs,
        in_specs=[vm],
        out_specs=[vm] * len(outs),
        compiler_params=pltpu.CompilerParams(vmem_limit_bytes=32 * 2**20),
    )(latent)


def weights_kernel(w, out):
    u = [[w[3 * i + j].astype(F32) for j in range(3)] for i in range(3)]
    for a in range(2):
        for da in range(2):
            if a == 0:
                row = u[0] if da == 0 else [x + y for x, y in zip(u[1], u[2])]
            else:
                row = u[2] if da == 1 else [x + y for x, y in zip(u[0], u[1])]
            for b in range(2):
                pair = (row[0], row[1] + row[2]) if b == 0 else (row[0] + row[1], row[2])
                for db in range(2):
                    out[((a * 2 + b) * 2 + da) * 2 + db] = pair[db].astype(BF16)


def phase_weights(w):
    taps, c1, c2 = w.shape
    step = 64
    return pl.pallas_call(
        weights_kernel,
        grid=(c1 // step,),
        out_shape=jax.ShapeDtypeStruct((16, c1, c2), BF16),
        in_specs=[pl.BlockSpec((taps, step, c2), lambda i: (0, i, 0))],
        out_specs=pl.BlockSpec((16, step, c2), lambda i: (0, i, 0)),
        compiler_params=pltpu.CompilerParams(vmem_limit_bytes=16 * 2**20),
        cost_estimate=pl.CostEstimate(
            flops=20 * c1 * c2, transcendentals=0, bytes_accessed=50 * c1 * c2
        ),
    )(w)


def face_kernel(p, n, second, *refs):
    outer, _ = messages(p, list(refs[:n]) + [None] * (p.peers - p.near))
    T = p.T
    odd = lax.bitwise_and(lax.axis_index("rows"), 1)
    to_above = odd == (0 if second else 1)
    out = refs[-1]

    @pl.when(to_above)
    def _():
        for f in range(p.F):
            out[f, 0:T] = outer[f][0:T, :]

    @pl.when(jnp.logical_not(to_above))
    def _():
        for f in range(p.F):
            out[f, 0:T] = outer[f][T + 8 : 2 * T + 8, :]

    for f in range(p.F):
        sums = outer[f][T : T + 8, :]
        out[f, T : T + 8] = sums
        if second:
            theirs = refs[n][f, T : T + 8]
            out[f, T + 8 : T + 16] = theirs


def face(p, got, first=None):
    vm = pl.BlockSpec(memory_space=pltpu.VMEM)
    rows = p.T + (8 if first is None else 16)
    args = list(got) + ([] if first is None else [first])
    return pl.pallas_call(
        functools.partial(face_kernel, p, len(got), first is not None),
        out_shape=jax.ShapeDtypeStruct((p.F, rows, p.c1), BF16),
        in_specs=[vm] * len(args),
        out_specs=vm,
        compiler_params=pltpu.CompilerParams(vmem_limit_bytes=16 * 2**20),
        cost_estimate=pl.CostEstimate(flops=1, transcendentals=0, bytes_accessed=1),
    )(*args)


def turner(p, first):
    F = p.F
    i = lax.broadcasted_iota(jnp.int32, (16 * F, 16 * F), 0)
    j = lax.broadcasted_iota(jnp.int32, (16 * F, 16 * F), 1)
    frame = lax.bitwise_xor(div(j, 16), first)
    return jnp.where((div(i, F) == mod(j, 16)) & (mod(i, F) == frame), 1.0, 0.0).astype(BF16)


def turn(p, load, matrix, scale, offset, block, runs, cells):
    if not any(max(f, block) < min(f + n, block + 16) for f, n, _ in runs):
        return
    data = jnp.concatenate([load(f, block) for f in range(p.F)], axis=0)
    turned = dot(matrix, data).reshape(16, p.F, p.c1)
    turned = silu(turned * scale[None] + offset[None])
    for first, count, row in runs:
        at, hi = max(first, block), min(first + count, block + 16)
        while at < hi:
            r, c = divmod(at - first, p.CH)
            n = min(hi - at, p.CH - c)
            cells[row + r, c : c + n] = turned[at - block : at - block + n]
            at += n


def clear_columns(p, cells, me):
    rows = cells.shape[0]

    @pl.when(me == 0)
    def _():
        cells[:, 0:2] = jnp.zeros((rows, 2, p.F, p.c1), F32)

    @pl.when(me == p.peers - 1)
    def _():
        cells[:, p.CH - 2 : p.CH] = jnp.zeros((rows, 2, p.F, p.c1), F32)


def pair_cells(p, row, even, odd):
    n = row.shape[0]
    even[...] = row.reshape(n // p.G, p.S, p.c1).astype(BF16)
    if p.G == 2:
        odd[...] = row[1 : n - 1].reshape(n // 2 - 1, p.S, p.c1).astype(BF16)


def shifted(p, rows, first, count, dc, n):
    parts = []
    for r in range(first, first + count) if isinstance(first, int) else first:
        even, odd = rows[r]
        if p.G == 1:
            v = even[dc : dc + n]
        elif dc == 1:
            v = odd[0:n]
        else:
            v = even[dc // 2 : dc // 2 + n]
        parts.append(v.reshape(n * p.S, p.c1))
    return jnp.concatenate(parts, axis=0)


def conv_one(p, out_rows, hidden, w1, b1, me, my_row, store):
    F, R, C, c1 = p.F, p.R, p.C, p.c1
    acc = None
    for dr in range(3):
        for dc in range(3):
            lhs = shifted(p, hidden, [r + dr for r in out_rows], 0, dc, (C + 2) // p.G)
            u = dot(lhs, w1[dr, dc])
            acc = u if acc is None else acc + u
    v = (acc + b1[...]).reshape(len(out_rows), C + 2, F, c1)
    left = jnp.where(me == 0, 1, 0)
    right = jnp.where(me == p.peers - 1, C + 1, C + 2)
    col = lax.broadcasted_iota(jnp.int32, (C + 2, F, c1), 0)
    for k, r in enumerate(out_rows):
        keep = (col >= left) & (col < right)
        if r == 0:
            keep = keep & (my_row > 0)
        if r == R + 1:
            keep = keep & (my_row < p.row_peers - 1)
        even, odd = store[r]
        pair_cells(p, jnp.where(keep, v[k], 0.0), even, odd)


def outer_kernel(p, n, *refs):
    outer, _ = messages(p, list(refs[:n]) + [None] * (p.peers - p.near))
    (face1, face2, gain, shift, w1, b1,
     norm, heven, hodd, feven, fodd, cells, teven, todd) = refs[n:]
    F, R, CH, T, c1 = p.F, p.R, p.CH, p.T, p.c1
    me = lax.axis_index("frames")
    my_row = lax.axis_index("rows")
    xor = me if p.swap else 0

    parts = jnp.concatenate(
        [outer[f][T : T + 8, :].astype(F32) for f in range(F)]
        + [face1[f, T : T + 8, :].astype(F32) for f in range(F)]
        + [face2[f, at : at + 8, :].astype(F32) for at in (T, T + 8) for f in range(F)],
        axis=0,
    ).astype(BF16)
    i = lax.broadcasted_iota(jnp.int32, (2 * F, parts.shape[0]), 0)
    j = lax.broadcasted_iota(jnp.int32, (2 * F, parts.shape[0]), 1)
    kind = mod(j, 8)
    wanted = jnp.where(i < F, jnp.where(kind < 3, 1, 0), jnp.where((kind >= 3) & (kind < 6), 1, 0))
    sent = lax.bitwise_xor(mod(div(j, 8), F), xor)
    pick = jnp.where((sent == mod(i, F)) & (wanted == 1), 1.0, 0.0).astype(BF16)
    sums = dot(pick, parts)
    per_group = c1 // GROUPS
    i = lax.broadcasted_iota(jnp.int32, (c1, c1), 0)
    j = lax.broadcasted_iota(jnp.int32, (c1, c1), 1)
    same = jnp.where(div(i, per_group) == div(j, per_group), 1.0, 0.0).astype(BF16)
    grouped = jnp.zeros((2 * F, c1), F32)
    for _ in range(3):
        term = sums.astype(BF16)
        grouped = grouped + dot(term, same)
        sums = sums - term.astype(F32)
    count = p.row_peers * R * p.W * per_group
    mean = grouped[:F] / count
    variance = grouped[F:] / count - mean * mean
    scale = lax.rsqrt(variance + GN_EPS) * gain[...]
    offset = shift[...] - mean * scale
    norm[0] = scale
    norm[1] = offset

    matrix = turner(p, xor)
    span = 2 * CH
    for block in sorted({min(b, p.NA - 16) for b in range(0, p.NA, 16)}):
        turn(p, lambda f, b: outer[f][b : b + 16, :], matrix, scale, offset, block,
             [(0, span, 2), (T + 8, span, 4)], cells)
    odd = lax.bitwise_and(my_row, 1)
    for block in range(0, span, 16):
        turn(p, lambda f, b: face1[f, b : b + 16, :], matrix, scale, offset, block,
             [(0, span, 6 - 6 * odd)], cells)
        turn(p, lambda f, b: face2[f, b : b + 16, :], matrix, scale, offset, block,
             [(0, span, 6 * odd)], cells)
    clear_columns(p, cells, me)

    @pl.when(my_row == 0)
    def _():
        cells[0:2] = jnp.zeros((2, CH, F, c1), F32)

    @pl.when(my_row == p.row_peers - 1)
    def _():
        cells[6:8] = jnp.zeros((2, CH, F, c1), F32)

    hidden = {}
    for k in range(8):
        if 2 <= k < 6:
            even, odd = heven.at[k - 2], hodd.at[k - 2]
        else:
            even, odd = teven.at[k % 4], todd.at[k % 4]
        pair_cells(p, cells[k], even, odd)
        hidden[k if k < 4 else R + k - 4] = (even, odd)
    rows = [0, 1, R, R + 1]
    store = {r: (feven.at[k], fodd.at[k]) for k, r in enumerate(rows)}
    conv_one(p, rows, hidden, w1, b1, me, my_row, store)


def inner_kernel(p, n, clip, *refs):
    _, inner = messages(p, list(refs[: p.near]) + [None] * (p.peers - p.near) + list(refs[p.near : n])
                        if p.swap else refs[:n])
    (norm, heven, hodd, feven_in, fodd_in, w1, w2, wt, b1, b2, bt, out,
     cells, even, odd, feven, fodd, phase, second, act, done, start, sems) = refs[n:]
    F, R, C, CH, S, c1, c2 = p.F, p.R, p.C, p.CH, p.S, p.c1, p.c2
    me = lax.axis_index("frames")
    my_row = lax.axis_index("rows")
    scale, offset = norm[0], norm[1]
    matrix = turner(p, me if p.swap else 0)
    for block in range(0, p.NB, 16):
        turn(p, lambda f, b: inner[f][b : b + 16, :], matrix, scale, offset, block,
             [(0, (R - 4) * CH, 0)], cells)
    clear_columns(p, cells, me)
    hidden = {r: (heven.at[k], hodd.at[k]) for k, r in enumerate((2, 3, R, R + 1))}
    for k in range(R - 4):
        hidden[4 + k] = (even.at[k], odd.at[k])
        pair_cells(p, cells[k], even.at[k], odd.at[k])
    first = {r: (feven_in.at[k], fodd_in.at[k]) for k, r in enumerate((0, 1, R, R + 1))}
    inside = {r: (feven.at[r - 2], fodd.at[r - 2]) for r in range(2, R)}
    conv_one(p, list(range(2, R)), hidden, w1, b1, me, my_row, inside)
    first.update(inside)

    for a in range(2):
        for b in range(2):
            acc = None
            for da in range(2):
                for db in range(2):
                    lhs = shifted(p, first, a + da, R, b + db, C // p.G)
                    u = dot(lhs, w2[((a * 2 + b) * 2 + da) * 2 + db])
                    acc = u if acc is None else acc + u
            phase[a, b] = (acc + b2[...]).astype(BF16).reshape(R, C * F, c2)

    q = p.q
    n = q * 2 * C
    i = lax.broadcasted_iota(jnp.int32, (n * F, n * F), 0)
    j = lax.broadcasted_iota(jnp.int32, (n * F, n * F), 1)
    source_cell = div(j, 2 * C * F) * (2 * C) + 2 * mod(div(j, F), C) + mod(div(j, C * F), 2)
    back = jnp.where((div(i, n) == mod(j, F)) & (mod(i, n) == source_cell), 1.0, 0.0).astype(BF16)
    for blk in range(2 * R // q):
        rows = range(blk * q, blk * q + q)
        x = jnp.concatenate([phase[o % 2, b, o // 2] for o in rows for b in range(2)], axis=0)
        turned = dot(back, x)
        second[:, blk * n : blk * n + n, :] = turned.astype(BF16).reshape(F, n, c2)
        act[:, blk * n : blk * n + n, :] = silu(turned).astype(BF16).reshape(F, n, c2)

    start[0] = 0

    def find(t, carry):
        start[t] = jnp.where(clip[t] == clip[t - 1], start[t - 1], t)
        return carry

    lax.fori_loop(1, F, find, 0)

    def temporal(t, carry):
        taps = [act[jnp.maximum(t - k * DILATION, start[t])] for k in range(TAPS)]
        lhs = jnp.concatenate(taps, axis=-1)
        done[t] = (dot(lhs, wt[...]) + second[t].astype(F32) + bt[...]).astype(BF16)
        pltpu.make_async_copy(done.at[t], out.at[t], sems.at[t]).start()
        return carry

    def finish(t, carry):
        pltpu.make_async_copy(done.at[t], out.at[t], sems.at[t]).wait()
        return carry

    if F <= 8:
        for t in range(F):
            temporal(t, 0)
        for t in range(F):
            finish(t, 0)
    else:
        lax.fori_loop(0, F, temporal, 0)
        lax.fori_loop(0, F, finish, 0)


def outer_rows(p, got, face1, face2, gain, shift, w1, b1):
    F, C, CH, G, S, c1 = p.F, p.C, p.CH, p.G, p.S, p.c1
    vm = pl.BlockSpec(memory_space=pltpu.VMEM)
    pairs = lambda rows, cells: [(rows, cells // G, S, c1), (rows, max(1, cells // G - 1), S, c1)]
    return pl.pallas_call(
        functools.partial(outer_kernel, p, len(got)),
        out_shape=[jax.ShapeDtypeStruct((2, F, c1), F32)]
        + [jax.ShapeDtypeStruct(s, BF16) for s in pairs(4, CH) + pairs(4, C + 2)],
        in_specs=[vm] * (len(got) + 6),
        out_specs=[vm] * 5,
        scratch_shapes=[pltpu.VMEM((8, CH, F, c1), F32)] + [pltpu.VMEM(s, BF16) for s in pairs(4, CH)],
        compiler_params=pltpu.CompilerParams(vmem_limit_bytes=p.vmem),
        cost_estimate=pl.CostEstimate(
            flops=2 * 9 * 4 * (C + 2) * F * c1 * c1, transcendentals=8 * CH * F * c1,
            bytes_accessed=2 * 9 * c1 * c1,
        ),
    )(*got, face1, face2, gain, shift, w1, b1)


def inner_rows(p, clip, got, norm, hidden, first, w1, w2, wt, b1, b2, bt):
    F, R, C, CH, G, S, c1, c2 = p.F, p.R, p.C, p.CH, p.G, p.S, p.c1, p.c2
    vm = pl.BlockSpec(memory_space=pltpu.VMEM)
    sm = pl.BlockSpec(memory_space=pltpu.SMEM)
    pairs = lambda rows, cells: [(rows, cells // G, S, c1), (rows, max(1, cells // G - 1), S, c1)]
    return pl.pallas_call(
        functools.partial(inner_kernel, p, len(got)),
        out_shape=jax.ShapeDtypeStruct((F, p.cells, c2), BF16),
        in_specs=[sm] + [vm] * (len(got) + 11),
        out_specs=pl.BlockSpec(memory_space=pl.ANY),
        scratch_shapes=[pltpu.VMEM((R - 4, CH, F, c1), F32)]
        + [pltpu.VMEM(s, BF16) for s in pairs(R - 4, CH) + pairs(R - 2, C + 2)]
        + [
            pltpu.VMEM((2, 2, R, C * F, c2), BF16),
            pltpu.VMEM((F, p.cells, c2), BF16),
            pltpu.VMEM((F, p.cells, c2), BF16),
            pltpu.VMEM((F, p.cells, c2), BF16),
            pltpu.SMEM((F,), jnp.int32),
            pltpu.SemaphoreType.DMA((F,)),
        ],
        compiler_params=pltpu.CompilerParams(vmem_limit_bytes=p.vmem),
        cost_estimate=pl.CostEstimate(
            flops=2 * (9 * (R - 2) * (C + 2) * c1 + 16 * R * C * c2) * F * c1,
            transcendentals=p.cells * F * c2, bytes_accessed=34 * c1 * c1,
        ),
    )(clip, *got, norm, *hidden, *first, w1, w2, wt, b1, b2, bt)


def per_device(
    latent, norm_gain, norm_shift, conv_one_w, bias_one, conv_two, bias_two,
    temporal_weight, bias_temporal, clip_ids,
):
    _, height, width, c1 = latent.shape
    c2 = conv_two.shape[-1]
    peers, row_peers = lax.axis_size("frames"), lax.axis_size("rows")
    p = Plan(clip_ids.shape[0], height, width // peers, width, c1, c2, row_peers)
    got = list(pack(p, latent[0]))
    far = range(p.near, peers)

    def swap(v, s):
        return lax.ppermute(v, "frames", [(i, i ^ s) for i in range(peers)])

    def after(v, k):
        v, got[k] = lax.optimization_barrier((v, got[k]))
        return v

    if p.swap:
        near, one, two = got[: p.near], got[p.near : peers], got[peers:]
        got = near + [swap(v, s) for v, s in zip(one, far)]
        for s in range(1, p.near):
            got[s] = swap(near[s], s)
        two = [swap(after(v, s), s) for v, s in zip(two, far)]
        last = got[: p.near] + two
    else:
        got = [lax.all_to_all(got[0], "frames", split_axis=0, concat_axis=0, tiled=True)]
        last = got

    def over_rows(v, *pairs):
        return lax.ppermute(v, "rows", [(i, j) for a, b in pairs for i, j in ((a, b), (b, a))])

    assert row_peers == 4
    w2 = phase_weights(conv_two.reshape(9, c1, c2))
    face1, w2 = lax.optimization_barrier((face(p, got), w2))
    face1 = over_rows(face1, (0, 1), (2, 3))
    face2 = over_rows(face(p, got, face1), (1, 2), (0, 3))
    w1 = conv_one_w.reshape(3, 3, c1, c1)
    norm, *packed = outer_rows(
        p, got, face1, face2, norm_gain[None], norm_shift[None], w1, bias_one[None]
    )
    out = inner_rows(
        p, clip_ids, last, norm, packed[:2], packed[2:], w1,
        w2, temporal_weight.reshape(TAPS * c2, c2),
        bias_one[None], bias_two[None], bias_temporal[None],
    )
    return out.reshape(p.F, 2 * height, 2 * p.C, c2)


def solution(mesh):
    in_specs = (P("frames", "rows", None, None), P(), P(), P(), P(), P(), P(), P(), P(), P())
    out_specs = P(None, "rows", "frames", None)
    return jax.shard_map(
        per_device, mesh=mesh, in_specs=in_specs, out_specs=out_specs, check_vma=False
    )
```

```python
import functools

import jax
import jax.numpy as jnp
from jax import lax
from jax.experimental import pallas as pl
from jax.experimental.pallas import tpu as pltpu
from jax.sharding import PartitionSpec as P

GROUPS = 32
TAPS = 3
DILATION = 2
GN_EPS = 1e-06
BF16, F32 = jnp.bfloat16, jnp.float32


def up_to(n, m):
    return -(-n // m) * m


class Plan:
    def __init__(self, frames, rows, cols, width, c1, c2, row_peers):
        self.F, self.R, self.C, self.W, self.c1, self.c2 = frames, rows, cols, width, c1, c2
        self.row_peers = row_peers
        self.peers = width // cols
        self.CH = cols + 4
        self.G = max(1, 16 // frames)
        self.S = self.G * frames
        self.T = up_to(2 * self.CH, 8)
        self.NA = 2 * self.T + 8
        self.NB = up_to((rows - 4) * self.CH, 16)
        self.q = max(1, 16 // (2 * cols))
        self.cells = 2 * rows * 2 * cols
        packed = (rows + 4) * self.CH * frames * c1
        self.vmem = 11 * packed + 24 * self.cells * frames * c2 // 2 + 4 * 2**20
        self.near = self.peers // 2
        self.swap = self.peers <= 8 and cols % 16 == 0


def silu(v):
    h = 0.5 * v
    return h + h * jnp.tanh(h)


def dot(a, b, **kw):
    return jnp.dot(a, b, preferred_element_type=F32, **kw)


def log2(n):
    assert n & (n - 1) == 0
    return n.bit_length() - 1


def div(x, n):
    return lax.shift_right_logical(x, log2(n))


def mod(x, n):
    return x & (n - 1)


def messages(p, refs):
    if not p.swap:
        whole = [refs[0].at[f] for f in range(p.peers)]
        return [r.at[: p.NA] for r in whole], [r.at[p.NA :] for r in whole]
    near, far = refs[: p.near], refs[p.near :]
    outer, inner = far[: p.peers - p.near], far[p.peers - p.near :]
    return (
        [r.at[: p.NA] for r in near] + list(outer),
        [r.at[p.NA :] for r in near] + list(inner),
    )


def in_three(total, square):
    parts = []
    for s in (total, square):
        high = s.astype(BF16).astype(F32)
        middle = (s - high).astype(BF16).astype(F32)
        parts += [high, middle, s - high - middle]
    return jnp.concatenate(parts + [jnp.zeros((2, s.shape[1]), F32)], axis=0).astype(BF16)


def pack_kernel(p, lat, *refs):
    R, C, W, CH, T = p.R, p.C, p.W, p.CH, p.T
    outer, inner = messages(p, refs)

    def row_static(r, dest):
        lo, hi = dest * C - 2, dest * C - 2 + CH
        v = lat[r, max(lo, 0) : min(hi, W), :]
        parts = []
        if lo < 0:
            parts.append(jnp.zeros((-lo, p.c1), BF16))
        parts.append(v)
        if hi > W:
            parts.append(jnp.zeros((hi - W, p.c1), BF16))
        return jnp.concatenate(parts, axis=0) if len(parts) > 1 else v

    def row_dynamic(r, dest):
        at = pl.multiple_of(dest * C, 16)
        before = pl.multiple_of(jnp.maximum(at - 16, 0), 16)
        after = pl.multiple_of(jnp.minimum(at + C, W - 16), 16)
        return jnp.concatenate(
            [lat[r, pl.ds(before, 16), :][14:], lat[r, pl.ds(at, C), :], lat[r, pl.ds(after, 16), :][:2]],
            axis=0,
        )

    total = jnp.zeros((1, p.c1), F32)
    square = jnp.zeros((1, p.c1), F32)
    for r in range(R):
        x = lat[r].astype(F32)
        total = total + jnp.sum(x, axis=0, keepdims=True)
        square = square + jnp.sum(x * x, axis=0, keepdims=True)
    parts = in_three(total, square)
    me = lax.axis_index("frames")
    for s in range(p.peers):
        a, b = outer[s], inner[s]
        if p.swap:
            load = functools.partial(row_dynamic, dest=lax.bitwise_xor(me, s))
        else:
            load = functools.partial(row_static, dest=s)
        for r, at in ((0, 0), (1, CH), (R - 2, T + 8), (R - 1, T + 8 + CH)):
            a[at : at + CH, :] = load(r)
        if 2 * CH < T:
            for at in (2 * CH, T + 8 + 2 * CH):
                a[at : at + T - 2 * CH, :] = jnp.zeros((T - 2 * CH, p.c1), BF16)
        a[T : T + 8, :] = parts
        for i in range(R - 4):
            b[i * CH : i * CH + CH, :] = load(2 + i)
        rest = (R - 4) * CH
        if rest < p.NB:
            b[rest : p.NB, :] = jnp.zeros((p.NB - rest, p.c1), BF16)


def pack(p, latent):
    vm = pl.BlockSpec(memory_space=pltpu.VMEM)
    n = p.NA + p.NB
    shapes = [(p.peers, n, p.c1)]
    if p.swap:
        far = p.peers - p.near
        shapes = [(n, p.c1)] * p.near + [(p.NA, p.c1)] * far + [(p.NB, p.c1)] * far
    outs = [jax.ShapeDtypeStruct(s, BF16) for s in shapes]
    return pl.pallas_call(
        functools.partial(pack_kernel, p),
        out_shape=outs,
        in_specs=[vm],
        out_specs=[vm] * len(outs),
        compiler_params=pltpu.CompilerParams(vmem_limit_bytes=32 * 2**20),
    )(latent)


def weights_kernel(w, out):
    u = [[w[3 * i + j].astype(F32) for j in range(3)] for i in range(3)]
    for a in range(2):
        for da in range(2):
            if a == 0:
                row = u[0] if da == 0 else [x + y for x, y in zip(u[1], u[2])]
            else:
                row = u[2] if da == 1 else [x + y for x, y in zip(u[0], u[1])]
            for b in range(2):
                pair = (row[0], row[1] + row[2]) if b == 0 else (row[0] + row[1], row[2])
                for db in range(2):
                    out[((a * 2 + b) * 2 + da) * 2 + db] = pair[db].astype(BF16)


def phase_weights(w):
    taps, c1, c2 = w.shape
    step = 64
    return pl.pallas_call(
        weights_kernel,
        grid=(c1 // step,),
        out_shape=jax.ShapeDtypeStruct((16, c1, c2), BF16),
        in_specs=[pl.BlockSpec((taps, step, c2), lambda i: (0, i, 0))],
        out_specs=pl.BlockSpec((16, step, c2), lambda i: (0, i, 0)),
        compiler_params=pltpu.CompilerParams(vmem_limit_bytes=16 * 2**20),
        cost_estimate=pl.CostEstimate(
            flops=20 * c1 * c2, transcendentals=0, bytes_accessed=50 * c1 * c2
        ),
    )(w)


def face_kernel(p, n, second, *refs):
    outer, _ = messages(p, list(refs[:n]) + [None] * (p.peers - p.near))
    T = p.T
    odd = lax.bitwise_and(lax.axis_index("rows"), 1)
    to_above = odd == (0 if second else 1)
    out = refs[-1]

    @pl.when(to_above)
    def _():
        for f in range(p.F):
            out[f, 0:T] = outer[f][0:T, :]

    @pl.when(jnp.logical_not(to_above))
    def _():
        for f in range(p.F):
            out[f, 0:T] = outer[f][T + 8 : 2 * T + 8, :]

    for f in range(p.F):
        sums = outer[f][T : T + 8, :]
        if second:
            both = sums.astype(F32) + refs[n][f, T : T + 8].astype(F32)
            sums = in_three(
                both[0:1] + both[1:2] + both[2:3], both[3:4] + both[4:5] + both[5:6]
            )
        out[f, T : T + 8] = sums


def face(p, got, first=None):
    vm = pl.BlockSpec(memory_space=pltpu.VMEM)
    rows = p.T + 8
    args = list(got) + ([] if first is None else [first])
    return pl.pallas_call(
        functools.partial(face_kernel, p, len(got), first is not None),
        out_shape=jax.ShapeDtypeStruct((p.F, rows, p.c1), BF16),
        in_specs=[vm] * len(args),
        out_specs=vm,
        compiler_params=pltpu.CompilerParams(vmem_limit_bytes=16 * 2**20),
        cost_estimate=pl.CostEstimate(flops=1, transcendentals=0, bytes_accessed=1),
    )(*args)


def turner(p, first):
    F = p.F
    i = lax.broadcasted_iota(jnp.int32, (16 * F, 16 * F), 0)
    j = lax.broadcasted_iota(jnp.int32, (16 * F, 16 * F), 1)
    frame = lax.bitwise_xor(div(j, 16), first)
    return jnp.where((div(i, F) == mod(j, 16)) & (mod(i, F) == frame), 1.0, 0.0).astype(BF16)


def turn(p, load, matrix, scale, offset, block, runs, cells):
    if not any(max(f, block) < min(f + n, block + 16) for f, n, _ in runs):
        return
    data = jnp.concatenate([load(f, block) for f in range(p.F)], axis=0)
    turned = dot(matrix, data).reshape(16, p.F, p.c1)
    turned = silu(turned * scale[None] + offset[None])
    for first, count, row in runs:
        at, hi = max(first, block), min(first + count, block + 16)
        while at < hi:
            r, c = divmod(at - first, p.CH)
            n = min(hi - at, p.CH - c)
            cells[row + r, c : c + n] = turned[at - block : at - block + n]
            at += n


def clear_columns(p, cells, me):
    rows = cells.shape[0]

    @pl.when(me == 0)
    def _():
        cells[:, 0:2] = jnp.zeros((rows, 2, p.F, p.c1), F32)

    @pl.when(me == p.peers - 1)
    def _():
        cells[:, p.CH - 2 : p.CH] = jnp.zeros((rows, 2, p.F, p.c1), F32)


def pair_cells(p, row, even, odd):
    n = row.shape[0]
    even[...] = row.reshape(n // p.G, p.S, p.c1).astype(BF16)
    if p.G == 2:
        odd[...] = row[1 : n - 1].reshape(n // 2 - 1, p.S, p.c1).astype(BF16)


def shifted(p, rows, first, count, dc, n):
    parts = []
    for r in range(first, first + count) if isinstance(first, int) else first:
        even, odd = rows[r]
        if p.G == 1:
            v = even[dc : dc + n]
        elif dc == 1:
            v = odd[0:n]
        else:
            v = even[dc // 2 : dc // 2 + n]
        parts.append(v.reshape(n * p.S, p.c1))
    return jnp.concatenate(parts, axis=0)


def conv_one(p, out_rows, hidden, w1, b1, me, my_row, store):
    F, R, C, c1 = p.F, p.R, p.C, p.c1
    acc = None
    for dr in range(3):
        for dc in range(3):
            lhs = shifted(p, hidden, [r + dr for r in out_rows], 0, dc, (C + 2) // p.G)
            u = dot(lhs, w1[dr, dc])
            acc = u if acc is None else acc + u
    v = (acc + b1[...]).reshape(len(out_rows), C + 2, F, c1)
    left = jnp.where(me == 0, 1, 0)
    right = jnp.where(me == p.peers - 1, C + 1, C + 2)
    col = lax.broadcasted_iota(jnp.int32, (C + 2, F, c1), 0)
    for k, r in enumerate(out_rows):
        keep = (col >= left) & (col < right)
        if r == 0:
            keep = keep & (my_row > 0)
        if r == R + 1:
            keep = keep & (my_row < p.row_peers - 1)
        even, odd = store[r]
        pair_cells(p, jnp.where(keep, v[k], 0.0), even, odd)


def outer_kernel(p, n, *refs):
    outer, _ = messages(p, list(refs[:n]) + [None] * (p.peers - p.near))
    (face1, face2, gain, shift, w1, b1,
     norm, heven, hodd, feven, fodd, cells, teven, todd) = refs[n:]
    F, R, CH, T, c1 = p.F, p.R, p.CH, p.T, p.c1
    me = lax.axis_index("frames")
    my_row = lax.axis_index("rows")
    xor = me if p.swap else 0

    parts = jnp.concatenate(
        [outer[f][T : T + 8, :].astype(F32) for f in range(F)]
        + [face1[f, T : T + 8, :].astype(F32) for f in range(F)]
        + [face2[f, T : T + 8, :].astype(F32) for f in range(F)],
        axis=0,
    ).astype(BF16)
    i = lax.broadcasted_iota(jnp.int32, (2 * F, parts.shape[0]), 0)
    j = lax.broadcasted_iota(jnp.int32, (2 * F, parts.shape[0]), 1)
    kind = mod(j, 8)
    wanted = jnp.where(i < F, jnp.where(kind < 3, 1, 0), jnp.where((kind >= 3) & (kind < 6), 1, 0))
    sent = lax.bitwise_xor(mod(div(j, 8), F), xor)
    pick = jnp.where((sent == mod(i, F)) & (wanted == 1), 1.0, 0.0).astype(BF16)
    sums = dot(pick, parts)
    per_group = c1 // GROUPS
    i = lax.broadcasted_iota(jnp.int32, (c1, c1), 0)
    j = lax.broadcasted_iota(jnp.int32, (c1, c1), 1)
    same = jnp.where(div(i, per_group) == div(j, per_group), 1.0, 0.0).astype(BF16)
    grouped = jnp.zeros((2 * F, c1), F32)
    for _ in range(3):
        term = sums.astype(BF16)
        grouped = grouped + dot(term, same)
        sums = sums - term.astype(F32)
    count = p.row_peers * R * p.W * per_group
    mean = grouped[:F] / count
    variance = grouped[F:] / count - mean * mean
    scale = lax.rsqrt(variance + GN_EPS) * gain[...]
    offset = shift[...] - mean * scale
    norm[0] = scale
    norm[1] = offset

    matrix = turner(p, xor)
    span = 2 * CH
    for block in sorted({min(b, p.NA - 16) for b in range(0, p.NA, 16)}):
        turn(p, lambda f, b: outer[f][b : b + 16, :], matrix, scale, offset, block,
             [(0, span, 2), (T + 8, span, 4)], cells)
    odd = lax.bitwise_and(my_row, 1)
    for block in range(0, span, 16):
        turn(p, lambda f, b: face1[f, b : b + 16, :], matrix, scale, offset, block,
             [(0, span, 6 - 6 * odd)], cells)
        turn(p, lambda f, b: face2[f, b : b + 16, :], matrix, scale, offset, block,
             [(0, span, 6 * odd)], cells)
    clear_columns(p, cells, me)

    @pl.when(my_row == 0)
    def _():
        cells[0:2] = jnp.zeros((2, CH, F, c1), F32)

    @pl.when(my_row == p.row_peers - 1)
    def _():
        cells[6:8] = jnp.zeros((2, CH, F, c1), F32)

    hidden = {}
    for k in range(8):
        if 2 <= k < 6:
            even, odd = heven.at[k - 2], hodd.at[k - 2]
        else:
            even, odd = teven.at[k % 4], todd.at[k % 4]
        pair_cells(p, cells[k], even, odd)
        hidden[k if k < 4 else R + k - 4] = (even, odd)
    rows = [0, 1, R, R + 1]
    store = {r: (feven.at[k], fodd.at[k]) for k, r in enumerate(rows)}
    conv_one(p, rows, hidden, w1, b1, me, my_row, store)


def inner_kernel(p, n, clip, *refs):
    _, inner = messages(p, list(refs[: p.near]) + [None] * (p.peers - p.near) + list(refs[p.near : n])
                        if p.swap else refs[:n])
    (norm, heven, hodd, feven_in, fodd_in, w1, w2, wt, b1, b2, bt, out,
     cells, even, odd, feven, fodd, phase, second, act, done, start, sems) = refs[n:]
    F, R, C, CH, S, c1, c2 = p.F, p.R, p.C, p.CH, p.S, p.c1, p.c2
    me = lax.axis_index("frames")
    my_row = lax.axis_index("rows")
    scale, offset = norm[0], norm[1]
    matrix = turner(p, me if p.swap else 0)
    for block in range(0, p.NB, 16):
        turn(p, lambda f, b: inner[f][b : b + 16, :], matrix, scale, offset, block,
             [(0, (R - 4) * CH, 0)], cells)
    clear_columns(p, cells, me)
    hidden = {r: (heven.at[k], hodd.at[k]) for k, r in enumerate((2, 3, R, R + 1))}
    for k in range(R - 4):
        hidden[4 + k] = (even.at[k], odd.at[k])
        pair_cells(p, cells[k], even.at[k], odd.at[k])
    first = {r: (feven_in.at[k], fodd_in.at[k]) for k, r in enumerate((0, 1, R, R + 1))}
    inside = {r: (feven.at[r - 2], fodd.at[r - 2]) for r in range(2, R)}
    conv_one(p, list(range(2, R)), hidden, w1, b1, me, my_row, inside)
    first.update(inside)

    for a in range(2):
        for b in range(2):
            acc = None
            for da in range(2):
                for db in range(2):
                    lhs = shifted(p, first, a + da, R, b + db, C // p.G)
                    u = dot(lhs, w2[((a * 2 + b) * 2 + da) * 2 + db])
                    acc = u if acc is None else acc + u
            phase[a, b] = (acc + b2[...]).astype(BF16).reshape(R, C * F, c2)

    q = p.q
    n = q * 2 * C
    i = lax.broadcasted_iota(jnp.int32, (n * F, n * F), 0)
    j = lax.broadcasted_iota(jnp.int32, (n * F, n * F), 1)
    source_cell = div(j, 2 * C * F) * (2 * C) + 2 * mod(div(j, F), C) + mod(div(j, C * F), 2)
    back = jnp.where((div(i, n) == mod(j, F)) & (mod(i, n) == source_cell), 1.0, 0.0).astype(BF16)
    for blk in range(2 * R // q):
        rows = range(blk * q, blk * q + q)
        x = jnp.concatenate([phase[o % 2, b, o // 2] for o in rows for b in range(2)], axis=0)
        turned = dot(back, x)
        second[:, blk * n : blk * n + n, :] = turned.astype(BF16).reshape(F, n, c2)
        act[:, blk * n : blk * n + n, :] = silu(turned).astype(BF16).reshape(F, n, c2)

    start[0] = 0

    def find(t, carry):
        start[t] = jnp.where(clip[t] == clip[t - 1], start[t - 1], t)
        return carry

    lax.fori_loop(1, F, find, 0)

    def temporal(t, carry):
        taps = [act[jnp.maximum(t - k * DILATION, start[t])] for k in range(TAPS)]
        lhs = jnp.concatenate(taps, axis=-1)
        done[t] = (dot(lhs, wt[...]) + second[t].astype(F32) + bt[...]).astype(BF16)
        pltpu.make_async_copy(done.at[t], out.at[t], sems.at[t]).start()
        return carry

    def finish(t, carry):
        pltpu.make_async_copy(done.at[t], out.at[t], sems.at[t]).wait()
        return carry

    if F <= 8:
        for t in range(F):
            temporal(t, 0)
        for t in range(F):
            finish(t, 0)
    else:
        lax.fori_loop(0, F, temporal, 0)
        lax.fori_loop(0, F, finish, 0)


def outer_rows(p, got, face1, face2, gain, shift, w1, b1):
    F, C, CH, G, S, c1 = p.F, p.C, p.CH, p.G, p.S, p.c1
    vm = pl.BlockSpec(memory_space=pltpu.VMEM)
    pairs = lambda rows, cells: [(rows, cells // G, S, c1), (rows, max(1, cells // G - 1), S, c1)]
    return pl.pallas_call(
        functools.partial(outer_kernel, p, len(got)),
        out_shape=[jax.ShapeDtypeStruct((2, F, c1), F32)]
        + [jax.ShapeDtypeStruct(s, BF16) for s in pairs(4, CH) + pairs(4, C + 2)],
        in_specs=[vm] * (len(got) + 6),
        out_specs=[vm] * 5,
        scratch_shapes=[pltpu.VMEM((8, CH, F, c1), F32)] + [pltpu.VMEM(s, BF16) for s in pairs(4, CH)],
        compiler_params=pltpu.CompilerParams(vmem_limit_bytes=p.vmem),
        cost_estimate=pl.CostEstimate(
            flops=2 * 9 * 4 * (C + 2) * F * c1 * c1, transcendentals=8 * CH * F * c1,
            bytes_accessed=2 * 9 * c1 * c1,
        ),
    )(*got, face1, face2, gain, shift, w1, b1)


def inner_rows(p, clip, got, norm, hidden, first, w1, w2, wt, b1, b2, bt):
    F, R, C, CH, G, S, c1, c2 = p.F, p.R, p.C, p.CH, p.G, p.S, p.c1, p.c2
    vm = pl.BlockSpec(memory_space=pltpu.VMEM)
    sm = pl.BlockSpec(memory_space=pltpu.SMEM)
    pairs = lambda rows, cells: [(rows, cells // G, S, c1), (rows, max(1, cells // G - 1), S, c1)]
    return pl.pallas_call(
        functools.partial(inner_kernel, p, len(got)),
        out_shape=jax.ShapeDtypeStruct((F, p.cells, c2), BF16),
        in_specs=[sm] + [vm] * (len(got) + 11),
        out_specs=pl.BlockSpec(memory_space=pl.ANY),
        scratch_shapes=[pltpu.VMEM((R - 4, CH, F, c1), F32)]
        + [pltpu.VMEM(s, BF16) for s in pairs(R - 4, CH) + pairs(R - 2, C + 2)]
        + [
            pltpu.VMEM((2, 2, R, C * F, c2), BF16),
            pltpu.VMEM((F, p.cells, c2), BF16),
            pltpu.VMEM((F, p.cells, c2), BF16),
            pltpu.VMEM((F, p.cells, c2), BF16),
            pltpu.SMEM((F,), jnp.int32),
            pltpu.SemaphoreType.DMA((F,)),
        ],
        compiler_params=pltpu.CompilerParams(vmem_limit_bytes=p.vmem),
        cost_estimate=pl.CostEstimate(
            flops=2 * (9 * (R - 2) * (C + 2) * c1 + 16 * R * C * c2) * F * c1,
            transcendentals=p.cells * F * c2, bytes_accessed=34 * c1 * c1,
        ),
    )(clip, *got, norm, *hidden, *first, w1, w2, wt, b1, b2, bt)


def per_device(
    latent, norm_gain, norm_shift, conv_one_w, bias_one, conv_two, bias_two,
    temporal_weight, bias_temporal, clip_ids,
):
    _, height, width, c1 = latent.shape
    c2 = conv_two.shape[-1]
    peers, row_peers = lax.axis_size("frames"), lax.axis_size("rows")
    p = Plan(clip_ids.shape[0], height, width // peers, width, c1, c2, row_peers)
    got = list(pack(p, latent[0]))
    far = range(p.near, peers)

    def swap(v, s):
        return lax.ppermute(v, "frames", [(i, i ^ s) for i in range(peers)])

    def after(v, k):
        v, got[k] = lax.optimization_barrier((v, got[k]))
        return v

    if p.swap:
        near, one, two = got[: p.near], got[p.near : peers], got[peers:]
        got = near + [swap(v, s) for v, s in zip(one, far)]
        for s in range(1, p.near):
            got[s] = swap(near[s], s)
        two = [swap(after(v, s), s) for v, s in zip(two, far)]
        last = got[: p.near] + two
    else:
        got = [lax.all_to_all(got[0], "frames", split_axis=0, concat_axis=0, tiled=True)]
        last = got

    def over_rows(v, *pairs):
        return lax.ppermute(v, "rows", [(i, j) for a, b in pairs for i, j in ((a, b), (b, a))])

    assert row_peers == 4
    w2 = phase_weights(conv_two.reshape(9, c1, c2))
    face1, w2 = lax.optimization_barrier((face(p, got), w2))
    face1 = over_rows(face1, (0, 1), (2, 3))
    face2 = over_rows(face(p, got, face1), (1, 2), (0, 3))
    w1 = conv_one_w.reshape(3, 3, c1, c1)
    norm, *packed = outer_rows(
        p, got, face1, face2, norm_gain[None], norm_shift[None], w1, bias_one[None]
    )
    out = inner_rows(
        p, clip_ids, last, norm, packed[:2], packed[2:], w1,
        w2, temporal_weight.reshape(TAPS * c2, c2),
        bias_one[None], bias_two[None], bias_temporal[None],
    )
    return out.reshape(p.F, 2 * height, 2 * p.C, c2)


def solution(mesh):
    in_specs = (P("frames", "rows", None, None), P(), P(), P(), P(), P(), P(), P(), P(), P())
    out_specs = P(None, "rows", "frames", None)
    return jax.shard_map(
        per_device, mesh=mesh, in_specs=in_specs, out_specs=out_specs, check_vma=False
    )
```

```python
import functools

import jax
import jax.numpy as jnp
from jax import lax
from jax.experimental import pallas as pl
from jax.experimental.pallas import tpu as pltpu
from jax.sharding import PartitionSpec as P

GROUPS = 32
TAPS = 3
DILATION = 2
GN_EPS = 1e-06
BF16, F32 = jnp.bfloat16, jnp.float32


def up_to(n, m):
    return -(-n // m) * m


class Plan:
    def __init__(self, frames, rows, cols, width, c1, c2, row_peers):
        self.F, self.R, self.C, self.W, self.c1, self.c2 = frames, rows, cols, width, c1, c2
        self.row_peers = row_peers
        self.peers = width // cols
        self.CH = cols + 4
        self.G = max(1, 16 // frames)
        self.S = self.G * frames
        self.T = up_to(2 * self.CH, 8)
        self.NA = 2 * self.T + 8
        self.NB = up_to((rows - 4) * self.CH, 16)
        self.q = max(1, 16 // (2 * cols))
        self.cells = 2 * rows * 2 * cols
        packed = (rows + 4) * self.CH * frames * c1
        self.vmem = 11 * packed + 24 * self.cells * frames * c2 // 2 + 4 * 2**20
        self.near = self.peers // 2
        self.swap = self.peers <= 8 and cols % 16 == 0


def silu(v):
    h = 0.5 * v
    return h + h * jnp.tanh(h)


def dot(a, b, **kw):
    return jnp.dot(a, b, preferred_element_type=F32, **kw)


def log2(n):
    assert n & (n - 1) == 0
    return n.bit_length() - 1


def div(x, n):
    return lax.shift_right_logical(x, log2(n))


def mod(x, n):
    return x & (n - 1)


def messages(p, refs):
    if not p.swap:
        whole = [refs[0].at[f] for f in range(p.peers)]
        return [r.at[: p.NA] for r in whole], [r.at[p.NA :] for r in whole]
    near, far = refs[: p.near], refs[p.near :]
    outer, inner = far[: p.peers - p.near], far[p.peers - p.near :]
    return (
        [r.at[: p.NA] for r in near] + list(outer),
        [r.at[p.NA :] for r in near] + list(inner),
    )


def pack_kernel(p, lat, *refs):
    R, C, W, CH, T = p.R, p.C, p.W, p.CH, p.T
    outer, inner = messages(p, refs)

    def row_static(r, dest):
        lo, hi = dest * C - 2, dest * C - 2 + CH
        v = lat[r, max(lo, 0) : min(hi, W), :]
        parts = []
        if lo < 0:
            parts.append(jnp.zeros((-lo, p.c1), BF16))
        parts.append(v)
        if hi > W:
            parts.append(jnp.zeros((hi - W, p.c1), BF16))
        return jnp.concatenate(parts, axis=0) if len(parts) > 1 else v

    def row_dynamic(r, dest):
        at = pl.multiple_of(dest * C, 16)
        before = pl.multiple_of(jnp.maximum(at - 16, 0), 16)
        after = pl.multiple_of(jnp.minimum(at + C, W - 16), 16)
        return jnp.concatenate(
            [lat[r, pl.ds(before, 16), :][14:], lat[r, pl.ds(at, C), :], lat[r, pl.ds(after, 16), :][:2]],
            axis=0,
        )

    total = jnp.zeros((1, p.c1), F32)
    square = jnp.zeros((1, p.c1), F32)
    for r in range(R):
        x = lat[r].astype(F32)
        total = total + jnp.sum(x, axis=0, keepdims=True)
        square = square + jnp.sum(x * x, axis=0, keepdims=True)
    parts = []
    for s in (total, square):
        high = s.astype(BF16).astype(F32)
        middle = (s - high).astype(BF16).astype(F32)
        parts += [high, middle, s - high - middle]
    parts = jnp.concatenate(parts + [jnp.zeros((2, p.c1), F32)], axis=0).astype(BF16)
    me = lax.axis_index("frames")
    for s in range(p.peers):
        a, b = outer[s], inner[s]
        if p.swap:
            load = functools.partial(row_dynamic, dest=lax.bitwise_xor(me, s))
        else:
            load = functools.partial(row_static, dest=s)
        for r, at in ((0, 0), (1, CH), (R - 2, T + 8), (R - 1, T + 8 + CH)):
            a[at : at + CH, :] = load(r)
        if 2 * CH < T:
            for at in (2 * CH, T + 8 + 2 * CH):
                a[at : at + T - 2 * CH, :] = jnp.zeros((T - 2 * CH, p.c1), BF16)
        a[T : T + 8, :] = parts
        for i in range(R - 4):
            b[i * CH : i * CH + CH, :] = load(2 + i)
        rest = (R - 4) * CH
        if rest < p.NB:
            b[rest : p.NB, :] = jnp.zeros((p.NB - rest, p.c1), BF16)


def pack(p, latent):
    vm = pl.BlockSpec(memory_space=pltpu.VMEM)
    n = p.NA + p.NB
    shapes = [(p.peers, n, p.c1)]
    if p.swap:
        far = p.peers - p.near
        shapes = [(n, p.c1)] * p.near + [(p.NA, p.c1)] * far + [(p.NB, p.c1)] * far
    outs = [jax.ShapeDtypeStruct(s, BF16) for s in shapes]
    return pl.pallas_call(
        functools.partial(pack_kernel, p),
        out_shape=outs,
        in_specs=[vm],
        out_specs=[vm] * len(outs),
        compiler_params=pltpu.CompilerParams(vmem_limit_bytes=32 * 2**20),
    )(latent)


def weights_kernel(w, out):
    u = [[w[3 * i + j].astype(F32) for j in range(3)] for i in range(3)]
    for a in range(2):
        for da in range(2):
            if a == 0:
                row = u[0] if da == 0 else [x + y for x, y in zip(u[1], u[2])]
            else:
                row = u[2] if da == 1 else [x + y for x, y in zip(u[0], u[1])]
            for b in range(2):
                pair = (row[0], row[1] + row[2]) if b == 0 else (row[0] + row[1], row[2])
                for db in range(2):
                    out[((a * 2 + b) * 2 + da) * 2 + db] = pair[db].astype(BF16)


def phase_weights(w):
    taps, c1, c2 = w.shape
    step = 64
    return pl.pallas_call(
        weights_kernel,
        grid=(c1 // step,),
        out_shape=jax.ShapeDtypeStruct((16, c1, c2), BF16),
        in_specs=[pl.BlockSpec((taps, step, c2), lambda i: (0, i, 0))],
        out_specs=pl.BlockSpec((16, step, c2), lambda i: (0, i, 0)),
        compiler_params=pltpu.CompilerParams(vmem_limit_bytes=16 * 2**20),
        cost_estimate=pl.CostEstimate(
            flops=20 * c1 * c2, transcendentals=0, bytes_accessed=50 * c1 * c2
        ),
    )(w)


def face_kernel(p, n, second, *refs):
    outer, _ = messages(p, list(refs[:n]) + [None] * (p.peers - p.near))
    T = p.T
    odd = lax.bitwise_and(lax.axis_index("rows"), 1)
    to_above = odd == (0 if second else 1)
    out = refs[-1]

    @pl.when(to_above)
    def _():
        for f in range(p.F):
            out[f, 0:T] = outer[f][0:T, :]

    @pl.when(jnp.logical_not(to_above))
    def _():
        for f in range(p.F):
            out[f, 0:T] = outer[f][T + 8 : 2 * T + 8, :]

    for f in range(p.F):
        sums = outer[f][T : T + 8, :]
        out[f, T : T + 8] = sums
        if second:
            theirs = refs[n][f, T : T + 8]
            out[f, T + 8 : T + 16] = theirs


def face(p, got, first=None):
    vm = pl.BlockSpec(memory_space=pltpu.VMEM)
    rows = p.T + (8 if first is None else 16)
    args = list(got) + ([] if first is None else [first])
    return pl.pallas_call(
        functools.partial(face_kernel, p, len(got), first is not None),
        out_shape=jax.ShapeDtypeStruct((p.F, rows, p.c1), BF16),
        in_specs=[vm] * len(args),
        out_specs=vm,
        compiler_params=pltpu.CompilerParams(vmem_limit_bytes=16 * 2**20),
        cost_estimate=pl.CostEstimate(flops=1, transcendentals=0, bytes_accessed=1),
    )(*args)


def turner(p, first):
    F = p.F
    i = lax.broadcasted_iota(jnp.int32, (16 * F, 16 * F), 0)
    j = lax.broadcasted_iota(jnp.int32, (16 * F, 16 * F), 1)
    frame = lax.bitwise_xor(div(j, 16), first)
    return jnp.where((div(i, F) == mod(j, 16)) & (mod(i, F) == frame), 1.0, 0.0).astype(BF16)


def turn(p, load, matrix, scale, offset, block, runs, cells):
    if not any(max(f, block) < min(f + n, block + 16) for f, n, _ in runs):
        return
    data = jnp.concatenate([load(f, block) for f in range(p.F)], axis=0)
    turned = dot(matrix, data).reshape(16, p.F, p.c1)
    turned = silu(turned * scale[None] + offset[None])
    for first, count, row in runs:
        at, hi = max(first, block), min(first + count, block + 16)
        while at < hi:
            r, c = divmod(at - first, p.CH)
            n = min(hi - at, p.CH - c)
            cells[row + r, c : c + n] = turned[at - block : at - block + n]
            at += n


def clear_columns(p, cells, me):
    rows = cells.shape[0]

    @pl.when(me == 0)
    def _():
        cells[:, 0:2] = jnp.zeros((rows, 2, p.F, p.c1), F32)

    @pl.when(me == p.peers - 1)
    def _():
        cells[:, p.CH - 2 : p.CH] = jnp.zeros((rows, 2, p.F, p.c1), F32)


def pair_cells(p, row, even, odd):
    n = row.shape[0]
    even[...] = row.reshape(n // p.G, p.S, p.c1).astype(BF16)
    if p.G == 2:
        odd[...] = row[1 : n - 1].reshape(n // 2 - 1, p.S, p.c1).astype(BF16)


def shifted(p, rows, first, count, dc, n):
    parts = []
    for r in range(first, first + count) if isinstance(first, int) else first:
        even, odd = rows[r]
        if p.G == 1:
            v = even[dc : dc + n]
        elif dc == 1:
            v = odd[0:n]
        else:
            v = even[dc // 2 : dc // 2 + n]
        parts.append(v.reshape(n * p.S, p.c1))
    return jnp.concatenate(parts, axis=0)


def conv_one(p, out_rows, hidden, w1, b1, me, my_row, store):
    F, R, C, c1 = p.F, p.R, p.C, p.c1
    acc = None
    for dr in range(3):
        for dc in range(3):
            lhs = shifted(p, hidden, [r + dr for r in out_rows], 0, dc, (C + 2) // p.G)
            u = dot(lhs, w1[dr, dc])
            acc = u if acc is None else acc + u
    v = (acc + b1[...]).reshape(len(out_rows), C + 2, F, c1)
    left = jnp.where(me == 0, 1, 0)
    right = jnp.where(me == p.peers - 1, C + 1, C + 2)
    col = lax.broadcasted_iota(jnp.int32, (C + 2, F, c1), 0)
    for k, r in enumerate(out_rows):
        keep = (col >= left) & (col < right)
        if r == 0:
            keep = keep & (my_row > 0)
        if r == R + 1:
            keep = keep & (my_row < p.row_peers - 1)
        even, odd = store[r]
        pair_cells(p, jnp.where(keep, v[k], 0.0), even, odd)


def outer_kernel(p, n, *refs):
    outer, _ = messages(p, list(refs[:n]) + [None] * (p.peers - p.near))
    (face1, face2, gain, shift, w1, b1,
     norm, heven, hodd, feven, fodd, cells, teven, todd) = refs[n:]
    F, R, CH, T, c1 = p.F, p.R, p.CH, p.T, p.c1
    me = lax.axis_index("frames")
    my_row = lax.axis_index("rows")
    xor = me if p.swap else 0

    parts = jnp.concatenate(
        [outer[f][T : T + 8, :].astype(F32) for f in range(F)]
        + [face1[f, T : T + 8, :].astype(F32) for f in range(F)]
        + [face2[f, at : at + 8, :].astype(F32) for at in (T, T + 8) for f in range(F)],
        axis=0,
    ).astype(BF16)
    i = lax.broadcasted_iota(jnp.int32, (2 * F, parts.shape[0]), 0)
    j = lax.broadcasted_iota(jnp.int32, (2 * F, parts.shape[0]), 1)
    kind = mod(j, 8)
    wanted = jnp.where(i < F, jnp.where(kind < 3, 1, 0), jnp.where((kind >= 3) & (kind < 6), 1, 0))
    sent = lax.bitwise_xor(mod(div(j, 8), F), xor)
    pick = jnp.where((sent == mod(i, F)) & (wanted == 1), 1.0, 0.0).astype(BF16)
    sums = dot(pick, parts)
    per_group = c1 // GROUPS
    i = lax.broadcasted_iota(jnp.int32, (c1, c1), 0)
    j = lax.broadcasted_iota(jnp.int32, (c1, c1), 1)
    same = jnp.where(div(i, per_group) == div(j, per_group), 1.0, 0.0).astype(BF16)
    grouped = jnp.zeros((2 * F, c1), F32)
    for _ in range(3):
        term = sums.astype(BF16)
        grouped = grouped + dot(term, same)
        sums = sums - term.astype(F32)
    count = p.row_peers * R * p.W * per_group
    mean = grouped[:F] / count
    variance = grouped[F:] / count - mean * mean
    scale = lax.rsqrt(variance + GN_EPS) * gain[...]
    offset = shift[...] - mean * scale
    norm[0] = scale
    norm[1] = offset

    matrix = turner(p, xor)
    span = 2 * CH
    for block in sorted({min(b, p.NA - 16) for b in range(0, p.NA, 16)}):
        turn(p, lambda f, b: outer[f][b : b + 16, :], matrix, scale, offset, block,
             [(0, span, 2), (T + 8, span, 4)], cells)
    odd = lax.bitwise_and(my_row, 1)
    for block in range(0, span, 16):
        turn(p, lambda f, b: face1[f, b : b + 16, :], matrix, scale, offset, block,
             [(0, span, 6 - 6 * odd)], cells)
        turn(p, lambda f, b: face2[f, b : b + 16, :], matrix, scale, offset, block,
             [(0, span, 6 * odd)], cells)
    clear_columns(p, cells, me)

    @pl.when(my_row == 0)
    def _():
        cells[0:2] = jnp.zeros((2, CH, F, c1), F32)

    @pl.when(my_row == p.row_peers - 1)
    def _():
        cells[6:8] = jnp.zeros((2, CH, F, c1), F32)

    hidden = {}
    for k in range(8):
        if 2 <= k < 6:
            even, odd = heven.at[k - 2], hodd.at[k - 2]
        else:
            even, odd = teven.at[k % 4], todd.at[k % 4]
        pair_cells(p, cells[k], even, odd)
        hidden[k if k < 4 else R + k - 4] = (even, odd)
    rows = [0, 1, R, R + 1]
    store = {r: (feven.at[k], fodd.at[k]) for k, r in enumerate(rows)}
    conv_one(p, rows, hidden, w1, b1, me, my_row, store)


def inner_kernel(p, n, clip, *refs):
    _, inner = messages(p, list(refs[: p.near]) + [None] * (p.peers - p.near) + list(refs[p.near : n])
                        if p.swap else refs[:n])
    (norm, heven, hodd, feven_in, fodd_in, w1, w2, wt, b1, b2, bt, out,
     cells, even, odd, feven, fodd, phase, second, act, done, start, sems) = refs[n:]
    F, R, C, CH, S, c1, c2 = p.F, p.R, p.C, p.CH, p.S, p.c1, p.c2
    me = lax.axis_index("frames")
    my_row = lax.axis_index("rows")
    scale, offset = norm[0], norm[1]
    matrix = turner(p, me if p.swap else 0)
    for block in range(0, p.NB, 16):
        turn(p, lambda f, b: inner[f][b : b + 16, :], matrix, scale, offset, block,
             [(0, (R - 4) * CH, 0)], cells)
    clear_columns(p, cells, me)
    hidden = {r: (heven.at[k], hodd.at[k]) for k, r in enumerate((2, 3, R, R + 1))}
    for k in range(R - 4):
        hidden[4 + k] = (even.at[k], odd.at[k])
        pair_cells(p, cells[k], even.at[k], odd.at[k])
    first = {r: (feven_in.at[k], fodd_in.at[k]) for k, r in enumerate((0, 1, R, R + 1))}
    inside = {r: (feven.at[r - 2], fodd.at[r - 2]) for r in range(2, R)}
    conv_one(p, list(range(2, R)), hidden, w1, b1, me, my_row, inside)
    first.update(inside)

    q = p.q
    n = q * 2 * C
    i = lax.broadcasted_iota(jnp.int32, (n * F, n * F), 0)
    j = lax.broadcasted_iota(jnp.int32, (n * F, n * F), 1)
    source_cell = div(j, 2 * C * F) * (2 * C) + 2 * mod(div(j, F), C) + mod(div(j, C * F), 2)
    back = jnp.where((div(i, n) == mod(j, F)) & (mod(i, n) == source_cell), 1.0, 0.0).astype(BF16)
    def to_frames(blk):
        rows = range(blk * q, blk * q + q)
        x = jnp.concatenate([phase[o % 2, b, o // 2] for o in rows for b in range(2)], axis=0)
        turned = dot(back, x)
        second[:, blk * n : blk * n + n, :] = turned.astype(BF16).reshape(F, n, c2)
        act[:, blk * n : blk * n + n, :] = silu(turned).astype(BF16).reshape(F, n, c2)

    for a in range(2):
        for b in range(2):
            acc = None
            for da in range(2):
                for db in range(2):
                    lhs = shifted(p, first, a + da, R, b + db, C // p.G)
                    u = dot(lhs, w2[((a * 2 + b) * 2 + da) * 2 + db])
                    acc = u if acc is None else acc + u
            phase[a, b] = (acc + b2[...]).astype(BF16).reshape(R, C * F, c2)
        if q == 1:
            for o in range(a, 2 * R, 2):
                to_frames(o)
    if q > 1:
        for blk in range(2 * R // q):
            to_frames(blk)

    start[0] = 0

    def find(t, carry):
        start[t] = jnp.where(clip[t] == clip[t - 1], start[t - 1], t)
        return carry

    lax.fori_loop(1, F, find, 0)

    def temporal(t, carry):
        taps = [act[jnp.maximum(t - k * DILATION, start[t])] for k in range(TAPS)]
        lhs = jnp.concatenate(taps, axis=-1)
        done[t] = (dot(lhs, wt[...]) + second[t].astype(F32) + bt[...]).astype(BF16)
        pltpu.make_async_copy(done.at[t], out.at[t], sems.at[t]).start()
        return carry

    def finish(t, carry):
        pltpu.make_async_copy(done.at[t], out.at[t], sems.at[t]).wait()
        return carry

    if F <= 8:
        for t in range(F):
            temporal(t, 0)
        for t in range(F):
            finish(t, 0)
    else:
        lax.fori_loop(0, F, temporal, 0)
        lax.fori_loop(0, F, finish, 0)


def outer_rows(p, got, face1, face2, gain, shift, w1, b1):
    F, C, CH, G, S, c1 = p.F, p.C, p.CH, p.G, p.S, p.c1
    vm = pl.BlockSpec(memory_space=pltpu.VMEM)
    pairs = lambda rows, cells: [(rows, cells // G, S, c1), (rows, max(1, cells // G - 1), S, c1)]
    return pl.pallas_call(
        functools.partial(outer_kernel, p, len(got)),
        out_shape=[jax.ShapeDtypeStruct((2, F, c1), F32)]
        + [jax.ShapeDtypeStruct(s, BF16) for s in pairs(4, CH) + pairs(4, C + 2)],
        in_specs=[vm] * (len(got) + 6),
        out_specs=[vm] * 5,
        scratch_shapes=[pltpu.VMEM((8, CH, F, c1), F32)] + [pltpu.VMEM(s, BF16) for s in pairs(4, CH)],
        compiler_params=pltpu.CompilerParams(vmem_limit_bytes=p.vmem),
        cost_estimate=pl.CostEstimate(
            flops=2 * 9 * 4 * (C + 2) * F * c1 * c1, transcendentals=8 * CH * F * c1,
            bytes_accessed=2 * 9 * c1 * c1,
        ),
    )(*got, face1, face2, gain, shift, w1, b1)


def inner_rows(p, clip, got, norm, hidden, first, w1, w2, wt, b1, b2, bt):
    F, R, C, CH, G, S, c1, c2 = p.F, p.R, p.C, p.CH, p.G, p.S, p.c1, p.c2
    vm = pl.BlockSpec(memory_space=pltpu.VMEM)
    sm = pl.BlockSpec(memory_space=pltpu.SMEM)
    pairs = lambda rows, cells: [(rows, cells // G, S, c1), (rows, max(1, cells // G - 1), S, c1)]
    return pl.pallas_call(
        functools.partial(inner_kernel, p, len(got)),
        out_shape=jax.ShapeDtypeStruct((F, p.cells, c2), BF16),
        in_specs=[sm] + [vm] * (len(got) + 11),
        out_specs=pl.BlockSpec(memory_space=pl.ANY),
        scratch_shapes=[pltpu.VMEM((R - 4, CH, F, c1), F32)]
        + [pltpu.VMEM(s, BF16) for s in pairs(R - 4, CH) + pairs(R - 2, C + 2)]
        + [
            pltpu.VMEM((2, 2, R, C * F, c2), BF16),
            pltpu.VMEM((F, p.cells, c2), BF16),
            pltpu.VMEM((F, p.cells, c2), BF16),
            pltpu.VMEM((F, p.cells, c2), BF16),
            pltpu.SMEM((F,), jnp.int32),
            pltpu.SemaphoreType.DMA((F,)),
        ],
        compiler_params=pltpu.CompilerParams(vmem_limit_bytes=p.vmem),
        cost_estimate=pl.CostEstimate(
            flops=2 * (9 * (R - 2) * (C + 2) * c1 + 16 * R * C * c2) * F * c1,
            transcendentals=p.cells * F * c2, bytes_accessed=34 * c1 * c1,
        ),
    )(clip, *got, norm, *hidden, *first, w1, w2, wt, b1, b2, bt)


def per_device(
    latent, norm_gain, norm_shift, conv_one_w, bias_one, conv_two, bias_two,
    temporal_weight, bias_temporal, clip_ids,
):
    _, height, width, c1 = latent.shape
    c2 = conv_two.shape[-1]
    peers, row_peers = lax.axis_size("frames"), lax.axis_size("rows")
    p = Plan(clip_ids.shape[0], height, width // peers, width, c1, c2, row_peers)
    got = list(pack(p, latent[0]))
    far = range(p.near, peers)

    def swap(v, s):
        return lax.ppermute(v, "frames", [(i, i ^ s) for i in range(peers)])

    def after(v, k):
        v, got[k] = lax.optimization_barrier((v, got[k]))
        return v

    if p.swap:
        near, one, two = got[: p.near], got[p.near : peers], got[peers:]
        got = near + [swap(v, s) for v, s in zip(one, far)]
        for s in range(1, p.near):
            got[s] = swap(near[s], s)
        two = [swap(after(v, s), s) for v, s in zip(two, far)]
        last = got[: p.near] + two
    else:
        got = [lax.all_to_all(got[0], "frames", split_axis=0, concat_axis=0, tiled=True)]
        last = got

    def over_rows(v, *pairs):
        return lax.ppermute(v, "rows", [(i, j) for a, b in pairs for i, j in ((a, b), (b, a))])

    assert row_peers == 4
    w2 = phase_weights(conv_two.reshape(9, c1, c2))
    face1, w2 = lax.optimization_barrier((face(p, got), w2))
    face1 = over_rows(face1, (0, 1), (2, 3))
    face2 = over_rows(face(p, got, face1), (1, 2), (0, 3))
    w1 = conv_one_w.reshape(3, 3, c1, c1)
    norm, *packed = outer_rows(
        p, got, face1, face2, norm_gain[None], norm_shift[None], w1, bias_one[None]
    )
    out = inner_rows(
        p, clip_ids, last, norm, packed[:2], packed[2:], w1,
        w2, temporal_weight.reshape(TAPS * c2, c2),
        bias_one[None], bias_two[None], bias_temporal[None],
    )
    return out.reshape(p.F, 2 * height, 2 * p.C, c2)


def solution(mesh):
    in_specs = (P("frames", "rows", None, None), P(), P(), P(), P(), P(), P(), P(), P(), P())
    out_specs = P(None, "rows", "frames", None)
    return jax.shard_map(
        per_device, mesh=mesh, in_specs=in_specs, out_specs=out_specs, check_vma=False
    )
```
